32 devices in a mesh: shard: 2 (over y), blk: 4 (over z), ckpt: 2 (over x), qry: 2 (over core).
Axes of the slice: x: 2, y: 2, z: 4, core: 2. Of those that a mesh axis runs over, the one named last changes fastest.
Arguments:
- query_feats: bfloat16 [2, 8192, 2048], P('ckpt', ('shard', 'blk', 'qry')), parts along dimension 1, may hold values from -6 to 6
- train_feats: bfloat16 [2, 1024, 2048], P('ckpt', ('shard', 'blk')), parts along dimension 1, may hold values from -0.125 to 0.125
- loss_weights: bfloat16 [2, 1024], P('ckpt', ('shard', 'blk')), parts along dimension 1, may hold values from 0.099609375 to 1
- pair_list: int32 [32, 2], P(('shard', 'blk', 'qry')), parts along dimension 0, may hold values from 0 to 3, all different within a row
- tile_owner: int32 [8], P('shard'), parts along dimension 0, may hold values from 0 to 3, each once
Outputs:
- scores: float32 [8192, 512], P(('shard', 'blk', 'qry'), 'ckpt'), parts along dimension 0
The draws below stay inside these ranges and needn't reach their ends.
There are 2 independent parts, one for each index of `shard`. The reference program is written for one: setup_inputs(seed, part) draws one part's arguments, and reference() takes and returns one part's arrays. A program takes and returns all parts, laid end to end along the dimension named above; each array names one. Nothing has to cross between parts.
Inputs may be any that keep to these rules, and one draw needn't show every extreme that they name: `pair_list`: each row names 2 different training blocks; every training block is named by some row. `tile_owner`: a permutation of the training blocks.
All inputs are finite; a program needn't handle non-finite values.
Results may differ from the reference program's by a relative error of at most 0.0003.
Values may be sent and summed in bfloat16 or wider, within the bound.
No kernel may reach another device: no remote copies, remote signals or barrier semaphores. Data moves between devices by JAX's collectives and lax.ppermute only.
A program may use at most 128 MiB of HBM per device.

```python
import math
import jax
import jax.numpy as jnp
from jax import lax

F = 2048
QBLK = 256
TBLK = 128
CKPT = 2
NTB = 4
NT = 512
NQB = 16
NQ = 4096
CAND = 2


def levels(own_key, dims, shards, least, top_value):
    def one(dim, parts):
        draws = jax.random.uniform(jax.random.fold_in(jax.random.fold_in(own_key, 6), dim), (parts,), jnp.float32, least / len(shards), top_value / len(shards))
        return jnp.repeat(jnp.exp(draws), dims[dim] // parts).reshape((-1,) + (1,) * (len(dims) - dim - 1))

    loudness = one(*shards[0])
    for cut in shards[1:]:
        loudness = loudness * one(*cut)
    return loudness


def distinct(stream_key, rows, amount, top, lift):
    sequence = jax.random.permutation(jax.random.fold_in(stream_key, 1), amount)
    boost = sequence
    for power in range(3):
        boost = boost * boost // amount
    boost = boost * lift // amount
    tickets = jax.random.randint(jax.random.fold_in(stream_key, 2), (rows, amount), 0, 4096) + boost
    sure = jax.random.permutation(jax.random.fold_in(stream_key, 3), rows)[jnp.arange(amount) % rows]
    tickets = jnp.where(jnp.arange(rows)[:, None] == sure[None, :], 1 << 14, tickets)
    priority = tickets * amount + jnp.arange(amount)
    return lax.top_k(priority.astype(jnp.int32), top)[1].astype(jnp.int32)


def gaussian(own_key, extent, spread, limit, shards=(), held_as=jnp.bfloat16):
    array = spread * jax.random.normal(own_key, extent, jnp.float32)
    if shards:
        array = array * levels(own_key, extent, shards, -0.22, 0.18)
    return jnp.clip(array, -limit, limit).astype(held_as)


def setup_inputs(seed: int = 0, part: int = 0) -> dict:
    keys = jax.random.split(jax.random.key(seed), 6)
    part_keys = jax.random.split(jax.random.fold_in(keys[5], part), 6)
    return {
        "query_feats": gaussian(part_keys[0], (CKPT, NQ, F), 1.0, 6.0, ((0, 2), (1, 8))),
        "train_feats": gaussian(part_keys[1], (CKPT, NT, F), F ** -0.5, 0.125, ((0, 2), (1, 4))),
        "loss_weights": jnp.clip(jnp.exp(math.log(1.0) - 2.306499 * jax.random.uniform(part_keys[2], (CKPT, NT), jnp.float32) ** levels(part_keys[2], (CKPT, NT), ((0, 2), (1, 4)), -0.2, 0.2)), 0.099609375, 1.0).astype(jnp.bfloat16),
        "pair_list": distinct(part_keys[3], NQB, NTB, CAND, 4096),
        "tile_owner": jax.random.permutation(part_keys[4], NTB).astype(jnp.int32),
    }


def reference(query_feats, train_feats, loss_weights, pair_list, tile_owner):
    block_ids = jnp.arange(NTB, dtype=jnp.int32)
    position = jnp.sum(jnp.where(tile_owner[None, :] == block_ids[:, None], block_ids[None, :], 0), axis=1).astype(jnp.int32)
    train_blocks = train_feats.reshape(CKPT, NTB, TBLK, F)
    weight_blocks = loss_weights.reshape(CKPT, NTB, TBLK)

    def score_block(query_block):
        chosen = pair_list[query_block]
        picked = train_blocks[:, chosen].astype(jnp.float32)
        weights = weight_blocks[:, chosen].astype(jnp.float32)
        queries = lax.dynamic_slice_in_dim(query_feats, (query_block * QBLK).astype(jnp.int32), QBLK, 1).astype(jnp.float32)
        terms = jnp.einsum("cqf,cktf->ckqt", queries, picked) * weights[:, :, None, :]
        summed = jnp.sum(terms, axis=0)
        placed = jnp.zeros((NTB, QBLK, TBLK), jnp.float32).at[position[chosen]].set(summed)
        return jnp.transpose(placed, (1, 0, 2)).reshape(QBLK, NT)

    rows = lax.map(score_block, jnp.arange(NQB, dtype=jnp.int32))
    return rows.reshape(NQ, NT)
```

```python
import functools

import jax
import jax.numpy as jnp
from jax import lax
from jax.experimental import pallas as pl
from jax.experimental.pallas import tpu as pltpu
from jax.sharding import PartitionSpec as P

CHUNKS = 2


def fold_ring(n):
    order = [2 * z for z in range(n)] + [2 * z + 1 for z in reversed(range(n))]
    return [(order[i], order[(i + 1) % len(order)]) for i in range(len(order))]


def shift(n, by):
    return [(i, (i + by) % n) for i in range(n)]


def xor(n, bit):
    return [(i, i ^ bit) for i in range(n)]


def whole(shape, dtype):
    return jax.ShapeDtypeStruct(shape, dtype)


VMEM = pl.BlockSpec(memory_space=pltpu.VMEM)
SMEM = pl.BlockSpec(memory_space=pltpu.SMEM)


def place_of(block, z, owner_ref, n, per):
    position = jnp.int32(0)
    for j in range(n):
        position = jnp.where(owner_ref[j] == block, j, position)
    owner = position // per
    slot = position % per
    mine = jnp.abs(block - z)
    rank = jnp.int32(0)
    for k in range(per):
        other = owner_ref[owner * per + k]
        far = jnp.abs(other - z)
        nearer = (far < mine) | ((far == mine) & (other < block))
        rank = rank + nearer.astype(jnp.int32)
    return owner, slot, rank


def score_into(put, sizes, block, rows, q_ref, w_ref, pair_ref, owner_ref):
    n, ckpts, per, nb, cand = sizes
    z = lax.axis_index("blk")
    c = lax.axis_index("ckpt")
    qblk = q_ref.shape[0] // nb

    @pl.when((block >= 0) & (block < n))
    def _():
        owner, slot, rank = place_of(block, z, owner_ref, n, per)
        away = lax.rem(owner - c + ckpts, ckpts)
        index = away * per + jnp.where(away == 0, slot, rank)
        weight = w_ref[pl.ds(block ^ z, 1), :]
        for b in range(nb):
            wanted = pair_ref[b, 0] == block
            for k in range(1, cand):
                wanted = wanted | (pair_ref[b, k] == block)

            @pl.when(wanted)
            def _():
                span = pl.ds(b * qblk, qblk)
                tile = lax.dot_general(
                    q_ref[span, :], rows(), (((1,), (1,)), ((), ())), preferred_element_type=jnp.float32
                )
                put(index, span, tile * weight)


def stacked(refs):
    if len(refs) == 1:
        return refs[0][...]
    return jnp.concatenate([ref[...] for ref in refs], axis=0)


def sources(dists, chunks, refs):
    z = lax.axis_index("blk")
    core = lax.axis_index("qry")
    at = 0
    for d in dists:
        if d == 0:
            yield z, refs[at : at + 1]
            at += 1
        else:
            yield z + jnp.where(core == 0, -d, d), refs[at : at + chunks]
            yield z + jnp.where(core == 0, d, -d), refs[at + chunks : at + 2 * chunks]
            at += 2 * chunks


def first_kernel(sizes, dists, chunks, pair_ref, owner_ref, w_ref, q_ref, *refs):
    n, ckpts, per, nb, cand = sizes
    count = 1 + 2 * chunks * (len(dists) - 1)
    ins, outs, terms = refs[:count], refs[count:-1], refs[-1]
    terms[...] = jnp.zeros_like(terms)

    def put(index, span, tile):
        terms[index, span, :] = tile

    for block, rows in sources(dists, chunks, ins):
        score_into(put, sizes, block, functools.partial(stacked, rows), q_ref, w_ref, pair_ref, owner_ref)
    width = terms.shape[2]
    for j in range(per):
        outs[0][:, j * width : (j + 1) * width] = terms[j]
    for i in range(per, ckpts * per):
        outs[1 + i - per][...] = terms[i]


def later_kernel(sizes, dist, chunks, pair_ref, owner_ref, w_ref, q_ref, *refs):
    n, ckpts, per, nb, cand = sizes
    rows_in = 2 * chunks
    outs = refs[rows_in + (len(refs) - rows_in) // 2 :]
    width = outs[1].shape[1]

    def put(index, span, tile):
        for i in range(ckpts * per):

            @pl.when(index == i)
            def _():
                if i < per:
                    outs[0][span, i * width : (i + 1) * width] = tile
                else:
                    outs[1 + i - per][span, :] = tile

    for i in range((len(refs) - rows_in) // 2):
        outs[i][...] = refs[rows_in + i][...]
    for block, rows in sources((dist,), chunks, refs[:rows_in]):
        score_into(put, sizes, block, functools.partial(stacked, rows), q_ref, w_ref, pair_ref, owner_ref)


def final_kernel(sizes, owner_ref, acc_ref, *refs):
    n, ckpts, per, nb, cand = sizes
    ins, out = refs[:-1], refs[-1]
    z = lax.axis_index("blk")
    c = lax.axis_index("ckpt")
    width = ins[0].shape[1]
    for j in range(per):
        owner, slot, rank = place_of(owner_ref[c * per + j], z, owner_ref, n, per)
        cols = slice(j * width, (j + 1) * width)
        for s in range(per):

            @pl.when(rank == s)
            def _():
                total = acc_ref[:, cols]
                for r in range(ckpts - 1):
                    total = total + ins[r * per + s][...]
                out[:, cols] = total


def per_device(query_feats, train_feats, loss_weights, pair_list, tile_owner):
    queries, own_rows, own_weights = query_feats[0], train_feats[0], loss_weights
    n, ckpts = lax.axis_size("blk"), lax.axis_size("ckpt")
    nb, cand = pair_list.shape
    per = n // ckpts
    rows = own_rows.shape[0]
    sizes = (n, ckpts, per, nb, cand)
    lines = ("blk", "qry")
    ring = fold_ring(n)
    swap = shift(2, 1)
    chunks = CHUNKS
    piece = rows // chunks

    held = [own_rows[i * piece : (i + 1) * piece] for i in range(chunks)]
    direct, crossed = [], []
    weights = own_weights.astype(jnp.float32)
    bit = 1
    for step in range(1, n):
        held = [lax.ppermute(part, lines, ring) for part in held]
        direct.append(held)
        crossed.append([lax.ppermute(part, "qry", swap) for part in held])
    while bit < n:
        weights = jnp.concatenate([weights, lax.ppermute(weights, "blk", xor(n, bit))], axis=0)
        bit *= 2

    queries_count = queries.shape[0]
    term = whole((queries_count, rows), jnp.float32)
    acc = whole((queries_count, per * rows), jnp.float32)
    ready = n - per
    near = [own_rows]
    for d in range(1, ready + 1):
        near += direct[d - 1] + crossed[d - 1]
    results = pl.pallas_call(
        functools.partial(first_kernel, sizes, tuple(range(ready + 1)), chunks),
        out_shape=[acc] + [term] * ((ckpts - 1) * per),
        in_specs=[SMEM, SMEM, VMEM, VMEM] + [VMEM] * len(near),
        out_specs=[VMEM] * (1 + (ckpts - 1) * per),
        scratch_shapes=[pltpu.VMEM((ckpts * per, queries_count, rows), jnp.float32)],
        name="near_scores",
    )(pair_list, tile_owner, weights, queries, *near)
    arrived = [None] * ((ckpts - 1) * per)
    for s in range(per):
        if s > 0:
            dist = ready + s
            news = direct[dist - 1] + crossed[dist - 1]
            results = pl.pallas_call(
                functools.partial(later_kernel, sizes, dist, chunks),
                out_shape=[acc] + [term] * ((ckpts - 1) * per),
                in_specs=[SMEM, SMEM, VMEM, VMEM] + [VMEM] * (len(news) + len(results)),
                out_specs=[VMEM] * len(results),
                name="far_scores",
            )(pair_list, tile_owner, weights, queries, *news, *results)
        for r in range(1, ckpts):
            at = (r - 1) * per + s
            arrived[at] = lax.ppermute(results[1 + at], "ckpt", shift(ckpts, r))
    return pl.pallas_call(
        functools.partial(final_kernel, sizes),
        out_shape=acc,
        in_specs=[SMEM, VMEM] + [VMEM] * len(arrived),
        out_specs=VMEM,
        name="sum_scores",
    )(tile_owner, results[0], *arrived)


def solution(mesh):
    return jax.shard_map(
        per_device,
        mesh=mesh,
        in_specs=(
            P("ckpt", ("shard", "blk", "qry"), None),
            P("ckpt", ("shard", "blk"), None),
            P("ckpt", ("shard", "blk")),
            P(("shard", "blk", "qry"), None),
            P("shard"),
        ),
        out_specs=P(("shard", "blk", "qry"), "ckpt"),
        check_vma=False,
    )
```

```python
import functools

import jax
import jax.numpy as jnp
from jax import lax
from jax.experimental import pallas as pl
from jax.experimental.pallas import tpu as pltpu
from jax.sharding import PartitionSpec as P


CHUNKS = 2
ANY = pl.BlockSpec(memory_space=pl.ANY)
VMEM = pl.BlockSpec(memory_space=pltpu.VMEM)
SMEM = pl.BlockSpec(memory_space=pltpu.SMEM)
LIMIT = 20 * 2**20


def fold_ring(n):
    order = [2 * z for z in range(n)] + [2 * z + 1 for z in reversed(range(n))]
    return [(order[i], order[(i + 1) % len(order)]) for i in range(len(order))]


def shift(n, by):
    return [(i, (i + by) % n) for i in range(n)]


def xor(n, bit):
    return [(i, i ^ bit) for i in range(n)]


def rank_of(block, z, owned):
    mine = jnp.abs(block - z)
    rank = jnp.int32(0)
    for other in owned:
        far = jnp.abs(other - z)
        nearer = (far < mine) | ((far == mine) & (other < block))
        rank = rank + nearer.astype(jnp.int32)
    return rank


def listed(pair_ref, b, block):
    wanted = pair_ref[b, 0] == block
    for k in range(1, pair_ref.shape[1]):
        wanted = wanted | (pair_ref[b, k] == block)
    return wanted


def sources(dists, chunks, refs):
    z = lax.axis_index("blk")
    core = lax.axis_index("qry")
    at = 0
    found = []
    for d in dists:
        if d == 0:
            found.append((z, refs[at : at + 1]))
            at += 1
        else:
            found.append((z + jnp.where(core == 0, -d, d), refs[at : at + chunks]))
            found.append((z + jnp.where(core == 0, d, -d), refs[at + chunks : at + 2 * chunks]))
            at += 2 * chunks
    return found


def fetch(block, pool, into, sem):
    for held, refs in pool:

        @pl.when(held == block)
        def _():
            piece = into.shape[0] // len(refs)
            for i, ref in enumerate(refs):
                pltpu.make_async_copy(ref, into.at[pl.ds(i * piece, piece)], sem).start()


def dot_rows(a, b):
    return lax.dot_general(a, b, (((1,), (1,)), ((), ())), preferred_element_type=jnp.float32)


def slot_kernel(n, ckpts, s, dists, chunks, pair_ref, owner_ref, w_ref, q_ref, *refs):
    per, nb = n // ckpts, pair_ref.shape[0]
    ins = refs[: -(ckpts - 1) - 2]
    outs = refs[-(ckpts - 1) - 2 : -2]
    rows, sem = refs[-2:]
    z, c = lax.axis_index("blk"), lax.axis_index("ckpt")
    qblk = q_ref.shape[0] // nb
    pool = sources(dists, chunks, ins)
    for r in range(1, ckpts):
        owner = lax.rem(c + r, ckpts)
        owned = [owner_ref[owner * per + k] for k in range(per)]
        block = jnp.int32(0)
        for one in owned:
            block = jnp.where(rank_of(one, z, owned) == s, one, block)
        fetch(block, pool, rows, sem)
        pltpu.make_async_copy(ins[0], rows, sem).wait()
        weight = w_ref[pl.ds(block ^ z, 1), :]
        for b in range(nb):
            span = pl.ds(b * qblk, qblk)
            wanted = listed(pair_ref, b, block)

            @pl.when(wanted)
            def _():
                outs[r - 1][span, :] = dot_rows(q_ref[span, :], rows[...]) * weight

            @pl.when(jnp.logical_not(wanted))
            def _():
                outs[r - 1][span, :] = jnp.zeros((qblk, rows.shape[0]), jnp.float32)


def own_kernel(n, ckpts, dists, chunks, pair_ref, owner_ref, w_ref, q_ref, *refs):
    per, nb = n // ckpts, pair_ref.shape[0]
    early = (per - 1) * (ckpts - 1)
    ins, came, out = refs[: len(refs) - early - 3], refs[len(refs) - early - 3 : -3], refs[-3]
    rows, sem = refs[-2:]
    z, c = lax.axis_index("blk"), lax.axis_index("ckpt")
    qblk = q_ref.shape[0] // nb
    width = rows.shape[1]
    pool = sources(dists, chunks, ins)
    owned = [owner_ref[c * per + k] for k in range(per)]
    for j, block in enumerate(owned):
        fetch(block, pool, rows.at[j], sem.at[j])
    for j, block in enumerate(owned):
        pltpu.make_async_copy(ins[0], rows.at[j], sem.at[j]).wait()
        cols = slice(j * width, (j + 1) * width)
        weight = w_ref[pl.ds(block ^ z, 1), :]
        for b in range(nb):
            span = pl.ds(b * qblk, qblk)
            wanted = listed(pair_ref, b, block)

            @pl.when(wanted)
            def _():
                out[span, cols] = dot_rows(q_ref[span, :], rows[j]) * weight

            @pl.when(jnp.logical_not(wanted))
            def _():
                out[span, cols] = jnp.zeros((qblk, width), jnp.float32)

        rank = rank_of(block, z, owned)
        for s in range(per - 1):

            @pl.when(rank == s)
            def _():
                for r in range(ckpts - 1):
                    out[:, cols] += came[s * (ckpts - 1) + r][...]


def sum_kernel(n, ckpts, owner_ref, acc_ref, *refs):
    per = n // ckpts
    came, out, tile, sem = refs[:-3], refs[-3], refs[-2], refs[-1]
    z, c = lax.axis_index("blk"), lax.axis_index("ckpt")
    width = tile.shape[1]
    owned = [owner_ref[c * per + k] for k in range(per)]
    last = jnp.int32(0)
    for j, block in enumerate(owned):
        last = jnp.where(rank_of(block, z, owned) == per - 1, j, last)
    cols = pl.ds(pl.multiple_of(last * width, width), width)
    load = pltpu.make_async_copy(acc_ref.at[:, cols], tile, sem)
    load.start()
    load.wait()
    total = tile[...]
    for part in came:
        total = total + part[...]
    tile[...] = total
    store = pltpu.make_async_copy(tile, out.at[:, cols], sem)
    store.start()
    store.wait()


def per_device(query_feats, train_feats, loss_weights, pair_list, tile_owner):
    queries, own_rows = query_feats[0], train_feats[0]
    n, ckpts = lax.axis_size("blk"), lax.axis_size("ckpt")
    per = n // ckpts
    rows, feats = own_rows.shape
    count = queries.shape[0]
    lines = ("blk", "qry")
    ring, swap = fold_ring(n), shift(2, 1)
    chunks, piece = CHUNKS, rows // CHUNKS

    held = [own_rows[i * piece : (i + 1) * piece] for i in range(chunks)]
    near = {0: [own_rows]}
    for step in range(1, n):
        held = [lax.ppermute(part, lines, ring) for part in held]
        near[step] = held + [lax.ppermute(part, "qry", swap) for part in held]
    weights = loss_weights.astype(jnp.float32)
    bit = 1
    while bit < n:
        weights = jnp.concatenate([weights, lax.ppermute(weights, "blk", xor(n, bit))], axis=0)
        bit *= 2

    tile = jax.ShapeDtypeStruct((count, rows), jnp.float32)
    acc = jax.ShapeDtypeStruct((count, per * rows), jnp.float32)
    params = pltpu.CompilerParams(vmem_limit_bytes=LIMIT)
    flops = 2 * count * rows * feats
    came = []
    for s in range(per):
        dists = tuple(range(n - per + s + 1))
        pool = [ref for d in dists for ref in near[d]]
        terms = pl.pallas_call(
            functools.partial(slot_kernel, n, ckpts, s, dists, chunks),
            out_shape=[tile] * (ckpts - 1),
            in_specs=[SMEM, SMEM, VMEM, VMEM] + [ANY] * len(pool),
            out_specs=[VMEM] * (ckpts - 1),
            scratch_shapes=[pltpu.VMEM((rows, feats), jnp.bfloat16), pltpu.SemaphoreType.DMA],
            compiler_params=params,
            cost_estimate=pl.CostEstimate(flops=flops * (ckpts - 1), bytes_accessed=count * feats * 2, transcendentals=0),
        )(pair_list, tile_owner, weights, queries, *pool)
        came.append([lax.ppermute(terms[r - 1], "ckpt", shift(ckpts, r)) for r in range(1, ckpts)])
    early = [part for parts in came[:-1] for part in parts]
    total = pl.pallas_call(
        functools.partial(own_kernel, n, ckpts, dists, chunks),
        out_shape=acc,
        in_specs=[SMEM, SMEM, VMEM, VMEM] + [ANY] * len(pool) + [VMEM] * len(early),
        out_specs=VMEM,
        scratch_shapes=[pltpu.VMEM((per, rows, feats), jnp.bfloat16), pltpu.SemaphoreType.DMA((per,))],
        compiler_params=params,
        cost_estimate=pl.CostEstimate(flops=flops * per, bytes_accessed=count * feats * 2, transcendentals=0),
    )(pair_list, tile_owner, weights, queries, *pool, *early)
    return pl.pallas_call(
        functools.partial(sum_kernel, n, ckpts),
        out_shape=acc,
        in_specs=[SMEM, ANY] + [VMEM] * (ckpts - 1),
        out_specs=ANY,
        input_output_aliases={1: 0},
        scratch_shapes=[pltpu.VMEM((count, rows), jnp.float32), pltpu.SemaphoreType.DMA],
        compiler_params=params,
    )(tile_owner, total, *came[-1])


def solution(mesh):
    return jax.shard_map(
        per_device,
        mesh=mesh,
        in_specs=(
            P("ckpt", ("shard", "blk", "qry"), None),
            P("ckpt", ("shard", "blk"), None),
            P("ckpt", ("shard", "blk")),
            P(("shard", "blk", "qry"), None),
            P("shard"),
        ),
        out_specs=P(("shard", "blk", "qry"), "ckpt"),
        check_vma=False,
    )
```

```python
import functools

import jax
import jax.numpy as jnp
from jax import lax
from jax.experimental import pallas as pl
from jax.experimental.pallas import tpu as pltpu
from jax.sharding import PartitionSpec as P


CHUNKS = 2
ANY = pl.BlockSpec(memory_space=pl.ANY)
VMEM = pl.BlockSpec(memory_space=pltpu.VMEM)
SMEM = pl.BlockSpec(memory_space=pltpu.SMEM)
LIMIT = 20 * 2**20
STEPS = 32767.0
TAIL = 16


def fold_ring(n):
    order = [2 * z for z in range(n)] + [2 * z + 1 for z in reversed(range(n))]
    return [(order[i], order[(i + 1) % len(order)]) for i in range(len(order))]


def shift(n, by):
    return [(i, (i + by) % n) for i in range(n)]


def xor(n, bit):
    return [(i, i ^ bit) for i in range(n)]


def rank_of(block, z, owned):
    mine = jnp.abs(block - z)
    rank = jnp.int32(0)
    for other in owned:
        far = jnp.abs(other - z)
        nearer = (far < mine) | ((far == mine) & (other < block))
        rank = rank + nearer.astype(jnp.int32)
    return rank


def pick_ranked(owned, z, s):
    block = owned[0]
    for one in owned[1:]:
        block = jnp.where(rank_of(one, z, owned) == s, one, block)
    return block


def scalars(n, nb, cand, refs):
    pairs = [[refs[b * cand + k] for k in range(cand)] for b in range(nb)]
    return pairs, [refs[nb * cand + j] for j in range(n)]


def pick(values, index):
    got = values[0]
    for k in range(1, len(values)):
        got = jnp.where(index == k, values[k], got)
    return got


def listed(pairs, b, block):
    wanted = pairs[b][0] == block
    for one in pairs[b][1:]:
        wanted = wanted | (one == block)
    return wanted


def sources(dists, chunks, refs):
    z = lax.axis_index("blk")
    core = lax.axis_index("qry")
    at = 0
    found = []
    for d in dists:
        directions = (0,) if d == 0 else (-d, d)
        for there in directions:
            found.append((z + jnp.where(core == 0, there, -there), refs[at : at + chunks]))
            at += chunks
    return found


def fetch(block, pool, into, sem):
    for held, refs in pool:

        @pl.when(held == block)
        def _():
            piece = into.shape[0] // len(refs)
            for i, ref in enumerate(refs):
                pltpu.make_async_copy(ref, into.at[pl.ds(i * piece, piece)], sem).start()


def dot_rows(a, b):
    return lax.dot_general(a, b, (((1,), (1,)), ((), ())), preferred_element_type=jnp.float32)


def coded(tile):
    top = jnp.maximum(jnp.max(jnp.abs(tile), axis=0, keepdims=True), 1e-36)
    power = jnp.ceil(jnp.log2(top))
    steps = jnp.clip(jnp.round(tile * jnp.exp2(-power) * STEPS), -STEPS, STEPS)
    return steps.astype(jnp.int32).astype(jnp.int16), power


def decoded(part, b, span, count):
    power = part[pl.ds(count, TAIL), :].astype(jnp.int32).astype(jnp.float32)[b : b + 1]
    steps = part[span, :].astype(jnp.int32).astype(jnp.float32)
    return steps * (jnp.exp2(power) * (1.0 / STEPS))


def load_kernel(q_ref, out):
    out[...] = q_ref[: out.shape[0], : out.shape[1]]


def slot_kernel(sizes, s, dists, chunks, packed, w_ref, q_ref, loaded, *refs):
    n, ckpts, per, nb, cand = sizes
    ins = refs[: -(ckpts - 1) - 2]
    outs = refs[-(ckpts - 1) - 2 : -2]
    rows, sem = refs[-2:]
    z, c = lax.axis_index("blk"), lax.axis_index("ckpt")
    pairs, order = scalars(n, nb, cand, packed)
    count = q_ref.shape[0]
    qblk, width = count // nb, rows.shape[0]
    pool = sources(dists, chunks, ins)
    for r in range(1, ckpts):
        owner = lax.rem(c + r, ckpts)
        owned = [pick(order[k::per], owner) for k in range(per)]
        block = pick_ranked(owned, z, s)
        fetch(block, pool, rows, sem)
        pltpu.make_async_copy(rows, rows, sem).wait()
        weight = w_ref[pl.ds(block ^ z, 1), :]
        out = outs[r - 1]
        out[pl.ds(count, TAIL), :] = jnp.zeros((TAIL, width), jnp.int16)
        for b in range(nb):
            span = pl.ds(b * qblk, qblk)
            wanted = listed(pairs, b, block)

            @pl.when(wanted)
            def _():
                steps, power = coded(dot_rows(q_ref[span, :], rows[...]) * weight)
                out[span, :] = steps
                line = lax.broadcasted_iota(jnp.int32, (TAIL, width), 0)
                old = out[pl.ds(count, TAIL), :].astype(jnp.int32)
                out[pl.ds(count, TAIL), :] = jnp.where(line == b, power.astype(jnp.int32), old).astype(jnp.int16)

            @pl.when(jnp.logical_not(wanted))
            def _():
                out[span, :] = jnp.zeros((qblk, width), jnp.int16)


def own_kernel(sizes, dists, chunks, packed, w_ref, q_ref, *refs):
    n, ckpts, per, nb, cand = sizes
    early = (per - 1) * (ckpts - 1)
    ins, came = refs[: len(refs) - early - 5], refs[len(refs) - early - 5 : -5]
    out, last, rows, tiles, sems = refs[-5:]
    z, c = lax.axis_index("blk"), lax.axis_index("ckpt")
    pairs, order = scalars(n, nb, cand, packed)
    count = q_ref.shape[0]
    qblk, width = count // nb, rows.shape[1]
    pool = sources(dists, chunks, ins)
    owned = [pick(order[k::per], c) for k in range(per)]
    ranked = [pick_ranked(owned, z, s) for s in range(per)]
    for s, block in enumerate(ranked):
        fetch(block, pool, rows.at[s], sems.at[s])
    for s, block in enumerate(ranked):
        pltpu.make_async_copy(rows.at[s], rows.at[s], sems.at[s]).wait()
        weight = w_ref[pl.ds(block ^ z, 1), :]
        into = last if s == per - 1 else tiles.at[s]
        for b in range(nb):
            span = pl.ds(b * qblk, qblk)
            wanted = listed(pairs, b, block)

            @pl.when(wanted)
            def _():
                total = dot_rows(q_ref[span, :], rows[s]) * weight
                if s < per - 1:
                    for r in range(ckpts - 1):
                        total = total + decoded(came[s * (ckpts - 1) + r], b, span, count)
                into[span, :] = total

            @pl.when(jnp.logical_not(wanted))
            def _():
                into[span, :] = jnp.zeros((qblk, width), jnp.float32)

        if s < per - 1:
            put_columns(tiles.at[s], out, owned, block, sems.at[s]).start()
    for s, block in enumerate(ranked[:-1]):
        put_columns(tiles.at[s], out, owned, block, sems.at[s]).wait()


def put_columns(tile, out, owned, block, sem):
    width = tile.shape[1]
    slot = jnp.int32(0)
    for j, one in enumerate(owned):
        slot = jnp.where(one == block, j, slot)
    return pltpu.make_async_copy(tile, out.at[:, pl.ds(pl.multiple_of(slot * width, width), width)], sem)


def sum_kernel(sizes, packed, acc_ref, last_ref, *refs):
    n, _, per, nb, cand = sizes
    came, out, tile, sem = refs[:-3], refs[-3], refs[-2], refs[-1]
    z, c = lax.axis_index("blk"), lax.axis_index("ckpt")
    _, order = scalars(n, nb, cand, packed)
    count = last_ref.shape[0]
    qblk = count // nb
    owned = [pick(order[k::per], c) for k in range(per)]
    block = pick_ranked(owned, z, per - 1)
    for b in range(nb):
        span = pl.ds(b * qblk, qblk)
        total = last_ref[span, :]
        for part in came:
            total = total + decoded(part, b, span, count)
        tile[span, :] = total
    store = put_columns(tile, out, owned, block, sem)
    store.start()
    store.wait()


def per_device(query_feats, train_feats, loss_weights, pair_list, tile_owner):
    queries, own_rows = query_feats[0], train_feats[0]
    n, ckpts = lax.axis_size("blk"), lax.axis_size("ckpt")
    per = n // ckpts
    rows, feats = own_rows.shape
    count = queries.shape[0]
    lines = ("blk", "qry")
    ring, swap = fold_ring(n), shift(2, 1)
    chunks, piece = CHUNKS, rows // CHUNKS

    params = pltpu.CompilerParams(vmem_limit_bytes=LIMIT)
    nb, cand = pair_list.shape
    sizes = (n, ckpts, per, nb, cand)
    held = [own_rows[i * piece : (i + 1) * piece] for i in range(chunks)]
    loaded = pl.pallas_call(
        load_kernel,
        out_shape=jax.ShapeDtypeStruct((8, rows), queries.dtype),
        in_specs=[VMEM],
        out_specs=VMEM,
        compiler_params=params,
    )(queries)
    packed = jnp.concatenate([pair_list.reshape(nb * cand), tile_owner])
    near = {0: held}
    weights = loss_weights
    for step in range(1, n):
        held = [lax.ppermute(part, lines, ring) for part in held]
        near[step] = held + [lax.ppermute(part, "qry", swap) for part in held]
    bit = 1
    while bit < n:
        weights = jnp.concatenate([weights, lax.ppermute(weights, "blk", xor(n, bit))], axis=0)
        bit *= 2
    weights = weights.astype(jnp.float32)

    sent = jax.ShapeDtypeStruct((count + TAIL, rows), jnp.int16)
    tile = jax.ShapeDtypeStruct((count, rows), jnp.float32)
    acc = jax.ShapeDtypeStruct((count, per * rows), jnp.float32)
    flops = 2 * count * rows * feats
    came = []
    for s in range(per):
        dists = tuple(range(n - per + s + 1))
        pool = [ref for d in dists for ref in near[d]]
        terms = pl.pallas_call(
            functools.partial(slot_kernel, sizes, s, dists, chunks),
            out_shape=[sent] * (ckpts - 1),
            in_specs=[SMEM, VMEM, VMEM, ANY] + [ANY] * len(pool),
            out_specs=[VMEM] * (ckpts - 1),
            scratch_shapes=[pltpu.VMEM((rows, feats), jnp.bfloat16), pltpu.SemaphoreType.DMA],
            compiler_params=params,
            cost_estimate=pl.CostEstimate(flops=flops * (ckpts - 1), bytes_accessed=count * feats * 2, transcendentals=0),
        )(packed, weights, queries, loaded, *pool)
        came.append([lax.ppermute(terms[r - 1], "ckpt", shift(ckpts, r)) for r in range(1, ckpts)])
    early = [part for parts in came[:-1] for part in parts]
    total, last = pl.pallas_call(
        functools.partial(own_kernel, sizes, dists, chunks),
        out_shape=[acc, tile],
        in_specs=[SMEM, VMEM, VMEM] + [ANY] * len(pool) + [VMEM] * len(early),
        out_specs=[ANY, VMEM],
        scratch_shapes=[
            pltpu.VMEM((per, rows, feats), jnp.bfloat16),
            pltpu.VMEM((max(per - 1, 1), count, rows), jnp.float32),
            pltpu.SemaphoreType.DMA((per,)),
        ],
        compiler_params=params,
        cost_estimate=pl.CostEstimate(flops=flops * per, bytes_accessed=count * feats * 2, transcendentals=0),
    )(packed, weights, queries, *pool, *early)
    return pl.pallas_call(
        functools.partial(sum_kernel, sizes),
        out_shape=acc,
        in_specs=[SMEM, ANY, VMEM] + [VMEM] * (ckpts - 1),
        out_specs=ANY,
        input_output_aliases={1: 0},
        scratch_shapes=[pltpu.VMEM((count, rows), jnp.float32), pltpu.SemaphoreType.DMA],
        compiler_params=params,
    )(packed, total, last, *came[-1])


def solution(mesh):
    return jax.shard_map(
        per_device,
        mesh=mesh,
        in_specs=(
            P("ckpt", ("shard", "blk", "qry"), None),
            P("ckpt", ("shard", "blk"), None),
            P("ckpt", ("shard", "blk")),
            P(("shard", "blk", "qry"), None),
            P("shard"),
        ),
        out_specs=P(("shard", "blk", "qry"), "ckpt"),
        check_vma=False,
    )
```

```python
import functools

import jax
import jax.numpy as jnp
from jax import lax
from jax.experimental import pallas as pl
from jax.experimental.pallas import tpu as pltpu
from jax.sharding import PartitionSpec as P


SPLIT = (1, 1)
ANY = pl.BlockSpec(memory_space=pl.ANY)
VMEM = pl.BlockSpec(memory_space=pltpu.VMEM)
SMEM = pl.BlockSpec(memory_space=pltpu.SMEM)
LIMIT = 20 * 2**20
STEPS = 32767.0
TAIL = 16


def fold_ring(n):
    order = [2 * z for z in range(n)] + [2 * z + 1 for z in reversed(range(n))]
    return [(order[i], order[(i + 1) % len(order)]) for i in range(len(order))]


def cuts(rows):
    unit = rows // sum(SPLIT)
    ends = [unit * sum(SPLIT[:i]) for i in range(len(SPLIT) + 1)]
    return [(a, b - a) for a, b in zip(ends, ends[1:])]


def shift(n, by):
    return [(i, (i + by) % n) for i in range(n)]


def rank_of(block, z, owned):
    mine = jnp.abs(block - z)
    rank = jnp.int32(0)
    for other in owned:
        far = jnp.abs(other - z)
        nearer = (far < mine) | ((far == mine) & (other < block))
        rank = rank + nearer.astype(jnp.int32)
    return rank


def pick_ranked(owned, z, s):
    block = owned[0]
    for one in owned[1:]:
        block = jnp.where(rank_of(one, z, owned) == s, one, block)
    return block


def scalars(n, nb, cand, refs):
    pairs = [[refs[b * cand + k] for k in range(cand)] for b in range(nb)]
    return pairs, [refs[nb * cand + j] for j in range(n)]


def pick(values, index):
    got = values[0]
    for k in range(1, len(values)):
        got = jnp.where(index == k, values[k], got)
    return got


def listed(pairs, b, block):
    wanted = pairs[b][0] == block
    for one in pairs[b][1:]:
        wanted = wanted | (one == block)
    return wanted


def sources(dists, chunks, refs):
    z = lax.axis_index("blk")
    core = lax.axis_index("qry")
    at = 0
    found = []
    for d in dists:
        directions = (0,) if d == 0 else (-d, d)
        for there in directions:
            found.append((z + jnp.where(core == 0, there, -there), refs[at : at + chunks]))
            at += chunks
    return found


def fetch(block, pool, into, w_into, sems):
    feats = into.shape[1]
    for held, refs in pool:

        @pl.when(held == block)
        def _():
            at = 0
            for ref in refs:
                rows = ref if ref.shape[1] == feats else ref.at[:, pl.ds(0, feats)]
                pltpu.make_async_copy(rows, into.at[pl.ds(at, ref.shape[0])], sems.at[0]).start()
                at += ref.shape[0]
            tail = refs[-1].at[pl.ds(0, TAIL), pl.ds(feats, w_into.shape[1])]
            pltpu.make_async_copy(tail, w_into, sems.at[1]).start()


def fetched(into, w_into, sems):
    pltpu.make_async_copy(into, into, sems.at[0]).wait()
    pltpu.make_async_copy(w_into, w_into, sems.at[1]).wait()
    return w_into[...].astype(jnp.float32)[:1]


def dot_rows(a, b):
    return lax.dot_general(a, b, (((1,), (1,)), ((), ())), preferred_element_type=jnp.float32)


def coded(tile):
    top = jnp.maximum(jnp.max(jnp.abs(tile), axis=0, keepdims=True), 1e-36)
    power = jnp.ceil(jnp.log2(top))
    steps = jnp.clip(jnp.round(tile * jnp.exp2(-power) * STEPS), -STEPS, STEPS)
    return steps.astype(jnp.int32).astype(jnp.int16), power


def decoded(part, b, span, count):
    power = part[pl.ds(count, TAIL), :].astype(jnp.int32).astype(jnp.float32)[b : b + 1]
    steps = part[span, :].astype(jnp.int32).astype(jnp.float32)
    return steps * (jnp.exp2(power) * (1.0 / STEPS))


def slot_kernel(sizes, s, dists, chunks, packed, *refs):
    n, ckpts, per, nb, cand = sizes
    qs, ins = refs[:nb], refs[nb : -(ckpts - 1) - 3]
    outs = refs[-(ckpts - 1) - 3 : -3]
    rows, w_rows, sems = refs[-3:]
    z, c = lax.axis_index("blk"), lax.axis_index("ckpt")
    pairs, order = scalars(n, nb, cand, packed)
    qblk, width = qs[0].shape[0], rows.shape[0]
    count = nb * qblk
    pool = sources(dists, chunks, ins)
    for r in range(1, ckpts):
        owner = lax.rem(c + r, ckpts)
        owned = [pick(order[k::per], owner) for k in range(per)]
        block = pick_ranked(owned, z, s)
        fetch(block, pool, rows, w_rows, sems)
        weight = fetched(rows, w_rows, sems)
        out = outs[r - 1]
        out[pl.ds(count, TAIL), :] = jnp.zeros((TAIL, width), jnp.int16)
        for b in range(nb):
            span = pl.ds(b * qblk, qblk)
            wanted = listed(pairs, b, block)

            @pl.when(wanted)
            def _():
                steps, power = coded(dot_rows(qs[b][...], rows[...]) * weight)
                out[span, :] = steps
                line = lax.broadcasted_iota(jnp.int32, (TAIL, width), 0)
                old = out[pl.ds(count, TAIL), :].astype(jnp.int32)
                out[pl.ds(count, TAIL), :] = jnp.where(line == b, power.astype(jnp.int32), old).astype(jnp.int16)

            @pl.when(jnp.logical_not(wanted))
            def _():
                out[span, :] = jnp.zeros((qblk, width), jnp.int16)


def own_kernel(sizes, dists, chunks, packed, *refs):
    n, ckpts, per, nb, cand = sizes
    early = (per - 1) * (ckpts - 1)
    qs, ins, came = refs[:nb], refs[nb : len(refs) - early - 6], refs[len(refs) - early - 6 : -6]
    out, last, rows, w_rows, tiles, sems = refs[-6:]
    z, c = lax.axis_index("blk"), lax.axis_index("ckpt")
    pairs, order = scalars(n, nb, cand, packed)
    qblk, width = qs[0].shape[0], rows.shape[1]
    count = nb * qblk
    pool = sources(dists, chunks, ins)
    owned = [pick(order[k::per], c) for k in range(per)]
    ranked = [pick_ranked(owned, z, s) for s in range(per)]
    for s, block in enumerate(ranked):
        fetch(block, pool, rows.at[s], w_rows.at[s], sems.at[s])
    for s, block in enumerate(ranked):
        weight = fetched(rows.at[s], w_rows.at[s], sems.at[s])
        into = last if s == per - 1 else tiles.at[s]
        for b in range(nb):
            span = pl.ds(b * qblk, qblk)
            wanted = listed(pairs, b, block)

            @pl.when(wanted)
            def _():
                total = dot_rows(qs[b][...], rows[s]) * weight
                if s < per - 1:
                    for r in range(ckpts - 1):
                        total = total + decoded(came[s * (ckpts - 1) + r], b, span, count)
                into[span, :] = total

            @pl.when(jnp.logical_not(wanted))
            def _():
                into[span, :] = jnp.zeros((qblk, width), jnp.float32)

        if s < per - 1:
            put_columns(tiles.at[s], out, owned, block, sems.at[s, 0]).start()
    for s, block in enumerate(ranked[:-1]):
        put_columns(tiles.at[s], out, owned, block, sems.at[s, 0]).wait()


def put_columns(tile, out, owned, block, sem, span=slice(None)):
    width = tile.shape[1]
    slot = jnp.int32(0)
    for j, one in enumerate(owned):
        slot = jnp.where(one == block, j, slot)
    columns = pl.ds(pl.multiple_of(slot * width, width), width)
    return pltpu.make_async_copy(tile.at[span, :], out.at[span, columns], sem)


def sum_kernel(sizes, packed, acc_ref, last_ref, *refs):
    n, _, per, nb, cand = sizes
    came, out, tile, sems = refs[:-3], refs[-3], refs[-2], refs[-1]
    z, c = lax.axis_index("blk"), lax.axis_index("ckpt")
    _, order = scalars(n, nb, cand, packed)
    count = last_ref.shape[0]
    qblk = count // nb
    owned = [pick(order[k::per], c) for k in range(per)]
    block = pick_ranked(owned, z, per - 1)
    stores = []
    for b in range(nb):
        span = pl.ds(b * qblk, qblk)
        total = last_ref[span, :]
        for part in came:
            total = total + decoded(part, b, span, count)
        tile[span, :] = total
        stores.append(put_columns(tile, out, owned, block, sems.at[b], span))
        stores[-1].start()
    for store in stores:
        store.wait()


def per_device(query_feats, train_feats, loss_weights, pair_list, tile_owner):
    queries, own_rows = query_feats[0], train_feats[0]
    n, ckpts = lax.axis_size("blk"), lax.axis_size("ckpt")
    per = n // ckpts
    rows, feats = own_rows.shape
    count = queries.shape[0]
    lines = ("blk", "qry")
    ring, swap = fold_ring(n), shift(2, 1)
    chunks = len(SPLIT)

    params = pltpu.CompilerParams(vmem_limit_bytes=LIMIT)
    nb, cand = pair_list.shape
    sizes = (n, ckpts, per, nb, cand)
    held = [own_rows[a : a + length] for a, length in cuts(rows)]
    tagged = jnp.broadcast_to(loss_weights, (held[-1].shape[0], rows))
    held[-1] = jnp.concatenate([held[-1], tagged], axis=1)
    packed = jnp.concatenate([pair_list.reshape(nb * cand), tile_owner])
    qblk = count // nb
    asked = []
    for b in range(nb):
        asked.append(queries[b * qblk : (b + 1) * qblk])
    near = {0: held}
    for step in range(1, n):
        held = [lax.ppermute(part, lines, ring) for part in held]
        near[step] = held + [lax.ppermute(part, "qry", swap) for part in held]
    sent = jax.ShapeDtypeStruct((count + TAIL, rows), jnp.int16)
    tile = jax.ShapeDtypeStruct((count, rows), jnp.float32)
    acc = jax.ShapeDtypeStruct((count, per * rows), jnp.float32)
    flops = 2 * count * rows * feats
    came = []
    for s in range(per):
        dists = tuple(range(n - per + s + 1))
        pool = [ref for d in dists for ref in near[d]]
        terms = pl.pallas_call(
            functools.partial(slot_kernel, sizes, s, dists, chunks),
            out_shape=[sent] * (ckpts - 1),
            in_specs=[SMEM] + [VMEM] * nb + [ANY] * len(pool),
            out_specs=[VMEM] * (ckpts - 1),
            scratch_shapes=[
                pltpu.VMEM((rows, feats), jnp.bfloat16),
                pltpu.VMEM((TAIL, rows), jnp.bfloat16),
                pltpu.SemaphoreType.DMA((2,)),
            ],
            compiler_params=params,
            cost_estimate=pl.CostEstimate(flops=flops * (ckpts - 1), bytes_accessed=count * feats * 2, transcendentals=0),
        )(packed, *asked, *pool)
        came.append([lax.ppermute(terms[r - 1], "ckpt", shift(ckpts, r)) for r in range(1, ckpts)])
    early = [part for parts in came[:-1] for part in parts]
    total, last = pl.pallas_call(
        functools.partial(own_kernel, sizes, dists, chunks),
        out_shape=[acc, tile],
        in_specs=[SMEM] + [VMEM] * nb + [ANY] * len(pool) + [VMEM] * len(early),
        out_specs=[ANY, VMEM],
        scratch_shapes=[
            pltpu.VMEM((per, rows, feats), jnp.bfloat16),
            pltpu.VMEM((per, TAIL, rows), jnp.bfloat16),
            pltpu.VMEM((max(per - 1, 1), count, rows), jnp.float32),
            pltpu.SemaphoreType.DMA((per, 2)),
        ],
        compiler_params=params,
        cost_estimate=pl.CostEstimate(flops=flops * per, bytes_accessed=count * feats * 2, transcendentals=0),
    )(packed, *asked, *pool, *early)
    return pl.pallas_call(
        functools.partial(sum_kernel, sizes),
        out_shape=acc,
        in_specs=[SMEM, ANY, VMEM] + [VMEM] * (ckpts - 1),
        out_specs=ANY,
        input_output_aliases={1: 0},
        scratch_shapes=[pltpu.VMEM((count, rows), jnp.float32), pltpu.SemaphoreType.DMA((nb,))],
        compiler_params=params,
    )(packed, total, last, *came[-1])


def solution(mesh):
    return jax.shard_map(
        per_device,
        mesh=mesh,
        in_specs=(
            P("ckpt", ("shard", "blk", "qry"), None),
            P("ckpt", ("shard", "blk"), None),
            P("ckpt", ("shard", "blk")),
            P(("shard", "blk", "qry"), None),
            P("shard"),
        ),
        out_specs=P(("shard", "blk", "qry"), "ckpt"),
        check_vma=False,
    )
```

```python
import functools

import jax
import jax.numpy as jnp
from jax import lax
from jax.experimental import pallas as pl
from jax.experimental.pallas import tpu as pltpu
from jax.sharding import PartitionSpec as P


SPLIT = (1, 1)
ANY = pl.BlockSpec(memory_space=pl.ANY)
VMEM = pl.BlockSpec(memory_space=pltpu.VMEM)
LIMIT = 20 * 2**20
STEPS = 32767.0
TAIL = 16


def fold_ring(n):
    order = [2 * z + 1 for z in range(n)] + [2 * z for z in reversed(range(n))]
    return [(order[i], order[(i + 1) % len(order)]) for i in range(len(order))]


def cuts(rows):
    unit = rows // sum(SPLIT)
    ends = [unit * sum(SPLIT[:i]) for i in range(len(SPLIT) + 1)]
    return [(a, b - a) for a, b in zip(ends, ends[1:])]


def shift(n, by):
    return [(i, (i + by) % n) for i in range(n)]


def rank_of(block, z, owned):
    mine = jnp.abs(block - z)
    rank = jnp.int32(0)
    for other in owned:
        far = jnp.abs(other - z)
        nearer = (far < mine) | ((far == mine) & (other < block))
        rank = rank + nearer.astype(jnp.int32)
    return rank


def pick_ranked(owned, z, s):
    block = owned[0]
    for one in owned[1:]:
        block = jnp.where(rank_of(one, z, owned) == s, one, block)
    return block


def scalars(n, nb, cand, refs):
    pairs = [[refs[0, b * cand + k] for k in range(cand)] for b in range(nb)]
    return pairs, [refs[0, nb * cand + j] for j in range(n)]


def pick(values, index):
    got = values[0]
    for k in range(1, len(values)):
        got = jnp.where(index == k, values[k], got)
    return got


def listed(pairs, b, block):
    wanted = pairs[b][0] == block
    for one in pairs[b][1:]:
        wanted = wanted | (one == block)
    return wanted


def sources(dists, chunks, refs):
    z = lax.axis_index("blk")
    core = lax.axis_index("qry")
    at = 0
    found = []
    for d in dists:
        directions = (0,) if d == 0 else (-d, d)
        for there in directions:
            found.append((z + jnp.where(core == 0, -there, there), refs[at : at + chunks]))
            at += chunks
    return found


def fetch(block, pool, into, w_into, sems):
    feats = into.shape[1]
    for held, refs in pool:

        @pl.when(held == block)
        def _():
            at = 0
            for ref in refs:
                rows = ref if ref.shape[1] == feats else ref.at[:, pl.ds(0, feats)]
                pltpu.make_async_copy(rows, into.at[pl.ds(at, ref.shape[0])], sems.at[0]).start()
                at += ref.shape[0]
            tail = refs[-1].at[pl.ds(0, TAIL), pl.ds(feats, w_into.shape[1])]
            pltpu.make_async_copy(tail, w_into, sems.at[1]).start()


def fetched(into, w_into, sems):
    pltpu.make_async_copy(into, into, sems.at[0]).wait()
    pltpu.make_async_copy(w_into, w_into, sems.at[1]).wait()
    return w_into[...].astype(jnp.float32)[:1]


def dot_rows(a, b):
    return lax.dot_general(a, b, (((1,), (1,)), ((), ())), preferred_element_type=jnp.float32)


def coded(tile):
    top = jnp.maximum(jnp.max(jnp.abs(tile), axis=0, keepdims=True), 1e-36)
    power = jnp.ceil(jnp.log2(top))
    steps = jnp.clip(jnp.round(tile * jnp.exp2(-power) * STEPS), -STEPS, STEPS)
    return steps.astype(jnp.int32).astype(jnp.int16), power


def decoded(part, b, span, count):
    power = part[pl.ds(count, TAIL), :].astype(jnp.int32).astype(jnp.float32)[b : b + 1]
    steps = part[span, :].astype(jnp.int32).astype(jnp.float32)
    return steps * (jnp.exp2(power) * (1.0 / STEPS))


def slot_kernel(sizes, s, dists, chunks, packed, *refs):
    n, ckpts, per, nb, cand = sizes
    qs, ins = refs[:nb], refs[nb : -(ckpts - 1) - 3]
    outs = refs[-(ckpts - 1) - 3 : -3]
    rows, w_rows, sems = refs[-3:]
    z, c = lax.axis_index("blk"), lax.axis_index("ckpt")
    pairs, order = scalars(n, nb, cand, packed)
    qblk, width = qs[0].shape[0], rows.shape[0]
    count = nb * qblk
    pool = sources(dists, chunks, ins)
    for r in range(1, ckpts):
        owner = lax.rem(c + r, ckpts)
        owned = [pick(order[k::per], owner) for k in range(per)]
        block = pick_ranked(owned, z, s)
        fetch(block, pool, rows, w_rows, sems)
        weight = fetched(rows, w_rows, sems)
        out = outs[r - 1]
        out[pl.ds(count, TAIL), :] = jnp.zeros((TAIL, width), jnp.int16)
        for b in range(nb):
            span = pl.ds(b * qblk, qblk)
            wanted = listed(pairs, b, block)

            @pl.when(wanted)
            def _():
                steps, power = coded(dot_rows(qs[b][...], rows[...]) * weight)
                out[span, :] = steps
                line = lax.broadcasted_iota(jnp.int32, (TAIL, width), 0)
                old = out[pl.ds(count, TAIL), :].astype(jnp.int32)
                out[pl.ds(count, TAIL), :] = jnp.where(line == b, power.astype(jnp.int32), old).astype(jnp.int16)

            @pl.when(jnp.logical_not(wanted))
            def _():
                out[span, :] = jnp.zeros((qblk, width), jnp.int16)


def own_kernel(sizes, dists, chunks, packed, *refs):
    n, ckpts, per, nb, cand = sizes
    early = (per - 1) * (ckpts - 1)
    qs, ins, came = refs[:nb], refs[nb : len(refs) - early - 6], refs[len(refs) - early - 6 : -6]
    out, last, rows, w_rows, tiles, sems = refs[-6:]
    z, c = lax.axis_index("blk"), lax.axis_index("ckpt")
    pairs, order = scalars(n, nb, cand, packed)
    qblk, width = qs[0].shape[0], rows.shape[1]
    count = nb * qblk
    pool = sources(dists, chunks, ins)
    owned = [pick(order[k::per], c) for k in range(per)]
    ranked = [pick_ranked(owned, z, s) for s in range(per)]
    for s, block in enumerate(ranked):
        fetch(block, pool, rows.at[s], w_rows.at[s], sems.at[s])
    for s, block in enumerate(ranked):
        weight = fetched(rows.at[s], w_rows.at[s], sems.at[s])
        into = last if s == per - 1 else tiles.at[s]
        for b in range(nb):
            span = pl.ds(b * qblk, qblk)
            wanted = listed(pairs, b, block)

            @pl.when(wanted)
            def _():
                total = dot_rows(qs[b][...], rows[s]) * weight
                if s < per - 1:
                    for r in range(ckpts - 1):
                        total = total + decoded(came[s * (ckpts - 1) + r], b, span, count)
                into[span, :] = total

            @pl.when(jnp.logical_not(wanted))
            def _():
                into[span, :] = jnp.zeros((qblk, width), jnp.float32)

        if s < per - 1:
            put_columns(tiles.at[s], out, owned, block, sems.at[s, 0]).start()
    for s, block in enumerate(ranked[:-1]):
        put_columns(tiles.at[s], out, owned, block, sems.at[s, 0]).wait()


def put_columns(tile, out, owned, block, sem, span=slice(None)):
    width = tile.shape[1]
    slot = jnp.int32(0)
    for j, one in enumerate(owned):
        slot = jnp.where(one == block, j, slot)
    columns = pl.ds(pl.multiple_of(slot * width, width), width)
    return pltpu.make_async_copy(tile.at[span, :], out.at[span, columns], sem)


def sum_kernel(sizes, packed, acc_ref, last_ref, *refs):
    n, _, per, nb, cand = sizes
    came, out, tile, sems = refs[:-3], refs[-3], refs[-2], refs[-1]
    z, c = lax.axis_index("blk"), lax.axis_index("ckpt")
    _, order = scalars(n, nb, cand, packed)
    count = last_ref.shape[0]
    qblk = count // nb
    owned = [pick(order[k::per], c) for k in range(per)]
    block = pick_ranked(owned, z, per - 1)
    stores = []
    for b in range(nb):
        span = pl.ds(b * qblk, qblk)
        total = last_ref[span, :]
        for part in came:
            total = total + decoded(part, b, span, count)
        tile[span, :] = total
        stores.append(put_columns(tile, out, owned, block, sems.at[b], span))
        stores[-1].start()
    for store in stores:
        store.wait()


def per_device(query_feats, train_feats, loss_weights, pair_list, tile_owner):
    queries, own_rows = query_feats[0], train_feats[0]
    n, ckpts = lax.axis_size("blk"), lax.axis_size("ckpt")
    per = n // ckpts
    rows, feats = own_rows.shape
    count = queries.shape[0]
    lines = ("blk", "qry")
    ring, swap = fold_ring(n), shift(2, 1)
    chunks = len(SPLIT)

    params = pltpu.CompilerParams(vmem_limit_bytes=LIMIT)
    nb, cand = pair_list.shape
    sizes = (n, ckpts, per, nb, cand)
    held = [own_rows[a : a + length] for a, length in cuts(rows)]
    tagged = jnp.broadcast_to(loss_weights, (held[-1].shape[0], rows))
    held[-1] = jnp.concatenate([held[-1], tagged], axis=1)
    packed = jnp.concatenate([pair_list.reshape(1, nb * cand), tile_owner[None, :]], axis=1)
    qblk = count // nb
    asked = []
    for b in range(nb):
        asked.append(queries[b * qblk : (b + 1) * qblk])
    near = {0: held}
    for step in range(1, n):
        held = [lax.ppermute(part, lines, ring) for part in held]
        near[step] = held + [lax.ppermute(part, "qry", swap) for part in held]
    sent = jax.ShapeDtypeStruct((count + TAIL, rows), jnp.int16)
    tile = jax.ShapeDtypeStruct((count, rows), jnp.float32)
    acc = jax.ShapeDtypeStruct((count, per * rows), jnp.float32)
    flops = 2 * count * rows * feats
    came = []
    for s in range(per):
        dists = tuple(range(n - per + s + 1))
        pool = [ref for d in dists for ref in near[d]]
        terms = pl.pallas_call(
            functools.partial(slot_kernel, sizes, s, dists, chunks),
            out_shape=[sent] * (ckpts - 1),
            in_specs=[VMEM] + [VMEM] * nb + [ANY] * len(pool),
            out_specs=[VMEM] * (ckpts - 1),
            scratch_shapes=[
                pltpu.VMEM((rows, feats), jnp.bfloat16),
                pltpu.VMEM((TAIL, rows), jnp.bfloat16),
                pltpu.SemaphoreType.DMA((2,)),
            ],
            compiler_params=params,
            cost_estimate=pl.CostEstimate(flops=flops * (ckpts - 1), bytes_accessed=count * feats * 2, transcendentals=0),
        )(packed, *asked, *pool)
        came.append([lax.ppermute(terms[r - 1], "ckpt", shift(ckpts, r)) for r in range(1, ckpts)])
    early = [part for parts in came[:-1] for part in parts]
    total, last = pl.pallas_call(
        functools.partial(own_kernel, sizes, dists, chunks),
        out_shape=[acc, tile],
        in_specs=[VMEM] + [VMEM] * nb + [ANY] * len(pool) + [VMEM] * len(early),
        out_specs=[ANY, VMEM],
        scratch_shapes=[
            pltpu.VMEM((per, rows, feats), jnp.bfloat16),
            pltpu.VMEM((per, TAIL, rows), jnp.bfloat16),
            pltpu.VMEM((max(per - 1, 1), count, rows), jnp.float32),
            pltpu.SemaphoreType.DMA((per, 2)),
        ],
        compiler_params=params,
        cost_estimate=pl.CostEstimate(flops=flops * per, bytes_accessed=count * feats * 2, transcendentals=0),
    )(packed, *asked, *pool, *early)
    return pl.pallas_call(
        functools.partial(sum_kernel, sizes),
        out_shape=acc,
        in_specs=[VMEM, ANY, VMEM] + [VMEM] * (ckpts - 1),
        out_specs=ANY,
        input_output_aliases={1: 0},
        scratch_shapes=[pltpu.VMEM((count, rows), jnp.float32), pltpu.SemaphoreType.DMA((nb,))],
        compiler_params=params,
    )(packed, total, last, *came[-1])


def solution(mesh):
    return jax.shard_map(
        per_device,
        mesh=mesh,
        in_specs=(
            P("ckpt", ("shard", "blk", "qry"), None),
            P("ckpt", ("shard", "blk"), None),
            P("ckpt", ("shard", "blk")),
            P(("shard", "blk", "qry"), None),
            P("shard"),
        ),
        out_specs=P(("shard", "blk", "qry"), "ckpt"),
        check_vma=False,
    )
```

```python
import functools

import jax
import jax.numpy as jnp
from jax import lax
from jax.experimental import pallas as pl
from jax.experimental.pallas import tpu as pltpu
from jax.sharding import PartitionSpec as P


SPLIT = (1, 1)
ANY = pl.BlockSpec(memory_space=pl.ANY)
VMEM = pl.BlockSpec(memory_space=pltpu.VMEM)
LIMIT = 20 * 2**20
STEPS = 32767.0
TAIL = 16
WEIGHT_STEPS = 16384.0


def fold_ring(n):
    order = [2 * z + 1 for z in range(n)] + [2 * z for z in reversed(range(n))]
    return [(order[i], order[(i + 1) % len(order)]) for i in range(len(order))]


def cuts(rows):
    unit = rows // sum(SPLIT)
    ends = [unit * sum(SPLIT[:i]) for i in range(len(SPLIT) + 1)]
    return [(a, b - a) for a, b in zip(ends, ends[1:])]


def shift(n, by):
    return [(i, (i + by) % n) for i in range(n)]


def rank_of(block, z, owned):
    mine = jnp.abs(block - z)
    rank = jnp.int32(0)
    for other in owned:
        far = jnp.abs(other - z)
        nearer = (far < mine) | ((far == mine) & (other < block))
        rank = rank + nearer.astype(jnp.int32)
    return rank


def pick_ranked(owned, z, s):
    block = owned[0]
    for one in owned[1:]:
        block = jnp.where(rank_of(one, z, owned) == s, one, block)
    return block


def scalars(n, nb, cand, refs):
    pairs = [[refs[0, b * cand + k] for k in range(cand)] for b in range(nb)]
    return pairs, [refs[0, nb * cand + j] for j in range(n)]


def pick(values, index):
    got = values[0]
    for k in range(1, len(values)):
        got = jnp.where(index == k, values[k], got)
    return got


def listed(pairs, b, block):
    wanted = pairs[b][0] == block
    for one in pairs[b][1:]:
        wanted = wanted | (one == block)
    return wanted


def sources(dists, chunks, refs):
    z = lax.axis_index("blk")
    core = lax.axis_index("qry")
    at = 0
    found = []
    for d in dists:
        directions = (0,) if d == 0 else (-d, d)
        for there in directions:
            found.append((z + jnp.where(core == 0, -there, there), refs[at : at + chunks]))
            at += chunks
    return found


def fetch(block, pool, into, w_into, sems):
    feats = into.shape[1]
    for held, refs in pool:

        @pl.when(held == block)
        def _():
            at = 0
            for ref in refs:
                rows = ref if ref.shape[1] == feats else ref.at[:, pl.ds(0, feats)]
                pltpu.make_async_copy(rows, into.at[pl.ds(at, ref.shape[0])], sems.at[0]).start()
                at += ref.shape[0]
            tail = refs[-1].at[pl.ds(0, TAIL), pl.ds(feats, w_into.shape[1])]
            pltpu.make_async_copy(tail, w_into, sems.at[1]).start()


def fetched(into, w_into, sems):
    pltpu.make_async_copy(into, into, sems.at[0]).wait()
    pltpu.make_async_copy(w_into, w_into, sems.at[1]).wait()
    return w_into[...].astype(jnp.float32)[:1]


def dot_rows(a, b):
    return lax.dot_general(a, b, (((1,), (1,)), ((), ())), preferred_element_type=jnp.float32)


def coded(tile):
    top = jnp.maximum(jnp.max(jnp.abs(tile), axis=0, keepdims=True), 1e-36)
    power = jnp.ceil(jnp.log2(top))
    steps = jnp.clip(jnp.round(tile * jnp.exp2(-power) * STEPS), -STEPS, STEPS)
    return steps.astype(jnp.int32).astype(jnp.int16), power


def decoded(part, b, span, count):
    power = part[pl.ds(count, TAIL), :].astype(jnp.int32).astype(jnp.float32)[b : b + 1]
    steps = part[span, :].astype(jnp.int32).astype(jnp.float32)
    return steps * (jnp.exp2(power) * (1.0 / STEPS))


def put_coded(out, b, span, count, tile):
    steps, power = coded(tile)
    out[span, :] = steps
    line = lax.broadcasted_iota(jnp.int32, (TAIL, tile.shape[1]), 0)
    old = out[pl.ds(count, TAIL), :].astype(jnp.int32)
    out[pl.ds(count, TAIL), :] = jnp.where(line == b, power.astype(jnp.int32), old).astype(jnp.int16)


def score_slot(pairs, block, qs, rows, weight, out):
    qblk, count = qs[0].shape[0], len(qs) * qs[0].shape[0]
    out[pl.ds(count, TAIL), :] = jnp.zeros((TAIL, out.shape[1]), jnp.int16)
    for b in range(len(qs)):
        span = pl.ds(b * qblk, qblk)
        wanted = listed(pairs, b, block)

        @pl.when(wanted)
        def _():
            put_coded(out, b, span, count, dot_rows(qs[b][...], rows[...]) * weight)

        @pl.when(jnp.logical_not(wanted))
        def _():
            out[span, :] = jnp.zeros((qblk, out.shape[1]), jnp.int16)


def slot_kernel(sizes, s, dists, chunks, packed, *refs):
    n, ckpts, per, nb, cand = sizes
    qs, ins = refs[:nb], refs[nb : -(ckpts - 1) - 3]
    outs = refs[-(ckpts - 1) - 3 : -3]
    rows, w_rows, sems = refs[-3:]
    z, c = lax.axis_index("blk"), lax.axis_index("ckpt")
    pairs, order = scalars(n, nb, cand, packed)
    pool = sources(dists, chunks, ins)
    for r in range(1, ckpts):
        owner = lax.rem(c + r, ckpts)
        block = pick_ranked([pick(order[k::per], owner) for k in range(per)], z, s)

        @pl.when(jnp.abs(block - z) <= dists[-1])
        def _():
            fetch(block, pool, rows, w_rows, sems)
            weight = fetched(rows, w_rows, sems)
            score_slot(pairs, block, qs, rows, weight, outs[r - 1])


def late_kernel(sizes, s, dist, chunks, packed, *refs):
    n, ckpts, per, nb, cand = sizes
    qs, ins = refs[:nb], refs[nb : nb + 2 * chunks]
    before, outs, rows = refs[nb + 2 * chunks : -ckpts], refs[-ckpts:-1], refs[-1]
    z, c = lax.axis_index("blk"), lax.axis_index("ckpt")
    pairs, order = scalars(n, nb, cand, packed)
    feats = rows.shape[1]
    for r in range(1, ckpts):
        owner = lax.rem(c + r, ckpts)
        block = pick_ranked([pick(order[k::per], owner) for k in range(per)], z, s)
        late = jnp.abs(block - z) == dist

        @pl.when(late)
        def _():
            weight = jnp.zeros((1, outs[0].shape[1]), jnp.float32)
            for held, parts in sources((dist,), chunks, ins):

                @pl.when(held == block)
                def _():
                    at = 0
                    for part in parts:
                        rows[pl.ds(at, part.shape[0]), :] = part[:, pl.ds(0, feats)]
                        at += part.shape[0]

                tail = parts[-1][pl.ds(0, TAIL), pl.ds(feats, outs[0].shape[1])].astype(jnp.float32)[:1]
                weight = jnp.where(held == block, tail, weight)
            score_slot(pairs, block, qs, rows, weight, outs[r - 1])

        @pl.when(jnp.logical_not(late))
        def _():
            outs[r - 1][...] = before[r - 1][...]


def regroup(tiles, index, width):
    group = lax.broadcasted_iota(jnp.int32, tiles[0].shape, 1) // width
    total = jnp.zeros_like(tiles[0])
    for k, tile in enumerate(tiles):
        by = (k - index) * width % tile.shape[1]
        total = total + jnp.where(group == k, pltpu.roll(tile, by, 1) if by else tile, 0.0)
    return total


def put_piece(tiles, out, weight):
    qblk = tiles[0].shape[0]
    tail = jnp.broadcast_to(jnp.round(weight * WEIGHT_STEPS), (TAIL, weight.shape[1])).astype(jnp.int32)
    line = lax.broadcasted_iota(jnp.int32, tail.shape, 0)
    for k, tile in enumerate(tiles):
        steps, power = coded(tile)
        out[pl.ds(k * qblk, qblk), :] = steps
        tail = jnp.where(line == k, power.astype(jnp.int32), tail)
    out[pl.ds(len(tiles) * qblk, TAIL), :] = tail.astype(jnp.int16)


def packed_pieces(part_refs, nb):
    chunks, width = len(part_refs), part_refs[0].shape[1]
    groups = nb // chunks
    qblk = (part_refs[0].shape[0] - TAIL) // groups
    tails = [ref[pl.ds(groups * qblk, TAIL), :].astype(jnp.int32).astype(jnp.float32) for ref in part_refs]
    weight = tails[-1][TAIL - 1 :] * (1.0 / WEIGHT_STEPS)
    found = []
    for b in range(nb):
        k = b // chunks
        tiles = []
        for ref, tail in zip(part_refs, tails):
            steps = ref[pl.ds(k * qblk, qblk), :].astype(jnp.int32).astype(jnp.float32)
            tiles.append(steps * (jnp.exp2(tail[k : k + 1]) * (1.0 / STEPS)))
        found.append(regroup(tiles, b % chunks, width // chunks) * weight)
    return found


def far_kernel(sizes, dists, chunks, packed, *refs):
    n, ckpts, per, nb, cand = sizes
    many = (ckpts - 1) * chunks
    qs, ins, outs = refs[:nb], refs[nb : -many - 4], refs[-many - 4 : -4]
    rows, w_rows, tiles, sems = refs[-4:]
    z, c = lax.axis_index("blk"), lax.axis_index("ckpt")
    pairs, order = scalars(n, nb, cand, packed)
    pool = sources(dists, chunks, ins)
    for r in range(1, ckpts):
        owner = lax.rem(c + r, ckpts)
        block = pick_ranked([pick(order[k::per], owner) for k in range(per)], z, per - 1)

        @pl.when(jnp.abs(block - z) <= dists[-1])
        def _():
            fetch(block, pool, rows, w_rows, sems)
            weight = fetched(rows, w_rows, sems)
            score_tiles(pairs, block, qs, rows, tiles)
            for i in range(chunks):
                groups = [
                    regroup([tiles[k * chunks + j] for j in range(chunks)], i, rows.shape[0] // chunks)
                    for k in range(nb // chunks)
                ]
                put_piece(groups, outs[(r - 1) * chunks + i], weight)


def score_tiles(pairs, block, qs, rows, tiles):
    for b in range(len(qs)):
        wanted = listed(pairs, b, block)

        @pl.when(wanted)
        def _():
            tiles[b] = dot_rows(qs[b][...], rows[...])

        @pl.when(jnp.logical_not(wanted))
        def _():
            tiles[b] = jnp.zeros_like(tiles[b])


def piece_kernel(sizes, i, dist, chunks, packed, *refs):
    n, ckpts, per, nb, cand = sizes
    qs, ins = refs[:nb], refs[nb : nb + 2]
    before, outs = refs[nb + 2 : nb + 1 + ckpts], refs[nb + 1 + ckpts : -2]
    rows, tiles = refs[-2:]
    z, c = lax.axis_index("blk"), lax.axis_index("ckpt")
    pairs, order = scalars(n, nb, cand, packed)
    width, feats = rows.shape
    piece = width // chunks
    for r in range(1, ckpts):
        owner = lax.rem(c + r, ckpts)
        block = pick_ranked([pick(order[k::per], owner) for k in range(per)], z, per - 1)
        late = jnp.abs(block - z) == dist

        @pl.when(late)
        def _():
            weight = jnp.ones((1, width), jnp.float32)
            for held, (part,) in sources((dist,), 1, ins):

                @pl.when(held == block)
                def _():
                    for j in range(chunks):
                        rows[pl.ds(j * piece, piece), :] = part[:, pl.ds(0, feats)]

                if i == chunks - 1:
                    tag = part[pl.ds(0, TAIL), pl.ds(feats, width)].astype(jnp.float32)[:1]
                    weight = jnp.where(held == block, tag, weight)
            score_tiles(pairs, block, qs, rows, tiles)
            group = lax.broadcasted_iota(jnp.int32, tiles.shape[1:], 1) // piece
            groups = []
            for k in range(nb // chunks):
                total = tiles[k * chunks]
                for j in range(1, chunks):
                    total = jnp.where(group == j, tiles[k * chunks + j], total)
                groups.append(total)
            put_piece(groups, outs[r - 1], weight)

        @pl.when(jnp.logical_not(late))
        def _():
            outs[r - 1][...] = before[r - 1][...]


def own_kernel(sizes, dists, chunks, packed, *refs):
    n, ckpts, per, nb, cand = sizes
    early = (per - 1) * (ckpts - 1)
    qs, ins, came = refs[:nb], refs[nb : len(refs) - early - 6], refs[len(refs) - early - 6 : -6]
    out, last, rows, w_rows, tiles, sems = refs[-6:]
    z, c = lax.axis_index("blk"), lax.axis_index("ckpt")
    pairs, order = scalars(n, nb, cand, packed)
    qblk, width = qs[0].shape[0], rows.shape[1]
    count = nb * qblk
    pool = sources(dists, chunks, ins)
    owned = [pick(order[k::per], c) for k in range(per)]
    ranked = [pick_ranked(owned, z, s) for s in range(per)]
    for s, block in enumerate(ranked):
        fetch(block, pool, rows.at[s], w_rows.at[s], sems.at[s])
    for s, block in enumerate(ranked):
        weight = fetched(rows.at[s], w_rows.at[s], sems.at[s])
        into = last if s == per - 1 else tiles.at[s]
        for b in range(nb):
            span = pl.ds(b * qblk, qblk)
            wanted = listed(pairs, b, block)

            @pl.when(wanted)
            def _():
                total = dot_rows(qs[b][...], rows[s]) * weight
                if s < per - 1:
                    for r in range(ckpts - 1):
                        total = total + decoded(came[s * (ckpts - 1) + r], b, span, count)
                into[span, :] = total

            @pl.when(jnp.logical_not(wanted))
            def _():
                into[span, :] = jnp.zeros((qblk, width), jnp.float32)

        if s < per - 1:
            put_columns(tiles.at[s], out, owned, block, sems.at[s, 0]).start()
    for s, block in enumerate(ranked[:-1]):
        put_columns(tiles.at[s], out, owned, block, sems.at[s, 0]).wait()


def put_columns(tile, out, owned, block, sem, span=slice(None)):
    width = tile.shape[1]
    slot = jnp.int32(0)
    for j, one in enumerate(owned):
        slot = jnp.where(one == block, j, slot)
    columns = pl.ds(pl.multiple_of(slot * width, width), width)
    return pltpu.make_async_copy(tile.at[span, :], out.at[span, columns], sem)


def sum_kernel(sizes, packed, acc_ref, last_ref, *refs):
    n, ckpts, per, nb, cand = sizes
    came, out, tile, sems = refs[:-3], refs[-3], refs[-2], refs[-1]
    z, c = lax.axis_index("blk"), lax.axis_index("ckpt")
    _, order = scalars(n, nb, cand, packed)
    count = last_ref.shape[0]
    qblk = count // nb
    owned = [pick(order[k::per], c) for k in range(per)]
    block = pick_ranked(owned, z, per - 1)
    stores = []
    chunks = len(came) // (ckpts - 1)
    parts = [packed_pieces(came[r * chunks : (r + 1) * chunks], nb) for r in range(ckpts - 1)]
    for b in range(nb):
        span = pl.ds(b * qblk, qblk)
        total = last_ref[span, :]
        for part in parts:
            total = total + part[b]
        tile[span, :] = total
        stores.append(put_columns(tile, out, owned, block, sems.at[b], span))
        stores[-1].start()
    for store in stores:
        store.wait()


def per_device(query_feats, train_feats, loss_weights, pair_list, tile_owner):
    queries, own_rows = query_feats[0], train_feats[0]
    n, ckpts = lax.axis_size("blk"), lax.axis_size("ckpt")
    per = n // ckpts
    rows, feats = own_rows.shape
    count = queries.shape[0]
    lines = ("blk", "qry")
    ring, swap = fold_ring(n), shift(2, 1)
    chunks = len(SPLIT)

    params = pltpu.CompilerParams(vmem_limit_bytes=LIMIT)
    nb, cand = pair_list.shape
    sizes = (n, ckpts, per, nb, cand)
    held = [own_rows[a : a + length] for a, length in cuts(rows)]
    tagged = jnp.broadcast_to(loss_weights, (held[-1].shape[0], rows))
    held[-1] = jnp.concatenate([held[-1], tagged], axis=1)
    packed = jnp.concatenate([pair_list.reshape(1, nb * cand), tile_owner[None, :]], axis=1)
    qblk = count // nb
    asked = []
    for b in range(nb):
        asked.append(queries[b * qblk : (b + 1) * qblk])
    near = {0: held}
    for step in range(1, n):
        held = [lax.ppermute(part, lines, ring) for part in held]
        near[step] = held + [lax.ppermute(part, "qry", swap) for part in held]
    sent = jax.ShapeDtypeStruct((count + TAIL, rows), jnp.int16)
    tile = jax.ShapeDtypeStruct((count, rows), jnp.float32)
    acc = jax.ShapeDtypeStruct((count, per * rows), jnp.float32)
    flops = 2 * count * rows * feats
    came = []
    cost = pl.CostEstimate(flops=flops * (ckpts - 1), bytes_accessed=count * feats * 2, transcendentals=0)
    for s in range(per - 1):
        seen = n - per + max(s - 1, 0)
        dists = tuple(range(seen + 1))
        pool = [ref for d in dists for ref in near[d]]
        terms = pl.pallas_call(
            functools.partial(slot_kernel, sizes, s, dists, chunks),
            out_shape=[sent] * (ckpts - 1),
            in_specs=[VMEM] + [VMEM] * nb + [ANY] * len(pool),
            out_specs=[VMEM] * (ckpts - 1),
            scratch_shapes=[
                pltpu.VMEM((rows, feats), jnp.bfloat16),
                pltpu.VMEM((TAIL, rows), jnp.bfloat16),
                pltpu.SemaphoreType.DMA((2,)),
            ],
            compiler_params=params,
            cost_estimate=cost,
        )(packed, *asked, *pool)
        if s > 0:
            terms = pl.pallas_call(
                functools.partial(late_kernel, sizes, s, seen + 1, chunks),
                out_shape=[sent] * (ckpts - 1),
                in_specs=[VMEM] + [VMEM] * (nb + 2 * chunks + ckpts - 1),
                out_specs=[VMEM] * (ckpts - 1),
                scratch_shapes=[pltpu.VMEM((rows, feats), jnp.bfloat16)],
                compiler_params=params,
                cost_estimate=cost,
            )(packed, *asked, *near[seen + 1], *terms)
        came.append([lax.ppermute(terms[r - 1], "ckpt", shift(ckpts, r)) for r in range(1, ckpts)])
    seen = n - 2
    dists = tuple(range(seen + 1))
    pool = [ref for d in dists for ref in near[d]]
    sent = jax.ShapeDtypeStruct((count // chunks + TAIL, rows), jnp.int16)
    tiles = pltpu.VMEM((nb, qblk, rows), jnp.float32)
    terms = pl.pallas_call(
        functools.partial(far_kernel, sizes, dists, chunks),
        out_shape=[sent] * ((ckpts - 1) * chunks),
        in_specs=[VMEM] * (1 + nb) + [ANY] * len(pool),
        out_specs=[VMEM] * ((ckpts - 1) * chunks),
        scratch_shapes=[
            pltpu.VMEM((rows, feats), jnp.bfloat16),
            pltpu.VMEM((TAIL, rows), jnp.bfloat16),
            tiles,
            pltpu.SemaphoreType.DMA((2,)),
        ],
        compiler_params=params,
        cost_estimate=cost,
    )(packed, *asked, *pool)
    pieces = {}
    for i in range(chunks):
        done = pl.pallas_call(
            functools.partial(piece_kernel, sizes, i, seen + 1, chunks),
            out_shape=[sent] * (ckpts - 1),
            in_specs=[VMEM] * (1 + nb + 2 + ckpts - 1),
            out_specs=[VMEM] * (ckpts - 1),
            scratch_shapes=[pltpu.VMEM((rows, feats), jnp.bfloat16), tiles],
            compiler_params=params,
            cost_estimate=cost,
        )(packed, *asked, near[seen + 1][i], near[seen + 1][chunks + i], *terms[i::chunks])
        for r in range(1, ckpts):
            pieces[r, i] = lax.ppermute(done[r - 1], "ckpt", shift(ckpts, r))
    came.append([pieces[r, i] for r in range(1, ckpts) for i in range(chunks)])
    dists = tuple(range(n))
    pool = [ref for d in dists for ref in near[d]]
    early = [part for parts in came[:-1] for part in parts]
    total, last = pl.pallas_call(
        functools.partial(own_kernel, sizes, dists, chunks),
        out_shape=[acc, tile],
        in_specs=[VMEM] + [VMEM] * nb + [ANY] * len(pool) + [VMEM] * len(early),
        out_specs=[ANY, VMEM],
        scratch_shapes=[
            pltpu.VMEM((per, rows, feats), jnp.bfloat16),
            pltpu.VMEM((per, TAIL, rows), jnp.bfloat16),
            pltpu.VMEM((max(per - 1, 1), count, rows), jnp.float32),
            pltpu.SemaphoreType.DMA((per, 2)),
        ],
        compiler_params=params,
        cost_estimate=pl.CostEstimate(flops=flops * per, bytes_accessed=count * feats * 2, transcendentals=0),
    )(packed, *asked, *pool, *early)
    return pl.pallas_call(
        functools.partial(sum_kernel, sizes),
        out_shape=acc,
        in_specs=[VMEM, ANY, VMEM] + [VMEM] * len(came[-1]),
        out_specs=ANY,
        input_output_aliases={1: 0},
        scratch_shapes=[pltpu.VMEM((count, rows), jnp.float32), pltpu.SemaphoreType.DMA((nb,))],
        compiler_params=params,
    )(packed, total, last, *came[-1])


def solution(mesh):
    return jax.shard_map(
        per_device,
        mesh=mesh,
        in_specs=(
            P("ckpt", ("shard", "blk", "qry"), None),
            P("ckpt", ("shard", "blk"), None),
            P("ckpt", ("shard", "blk")),
            P(("shard", "blk", "qry"), None),
            P("shard"),
        ),
        out_specs=P(("shard", "blk", "qry"), "ckpt"),
        check_vma=False,
    )
```

```python
import functools

import jax
import jax.numpy as jnp
from jax import lax
from jax.experimental import pallas as pl
from jax.experimental.pallas import tpu as pltpu
from jax.sharding import PartitionSpec as P


SPLIT = (1, 1)
ANY = pl.BlockSpec(memory_space=pl.ANY)
VMEM = pl.BlockSpec(memory_space=pltpu.VMEM)
LIMIT = 20 * 2**20
STEPS = 32767.0
TAIL = 16
WEIGHT_STEPS = 16384.0


def fold_ring(n):
    order = [2 * z + 1 for z in range(n)] + [2 * z for z in reversed(range(n))]
    return [(order[i], order[(i + 1) % len(order)]) for i in range(len(order))]


def cuts(rows):
    unit = rows // sum(SPLIT)
    ends = [unit * sum(SPLIT[:i]) for i in range(len(SPLIT) + 1)]
    return [(a, b - a) for a, b in zip(ends, ends[1:])]


def shift(n, by):
    return [(i, (i + by) % n) for i in range(n)]


def rank_of(block, z, owned):
    mine = jnp.abs(block - z)
    rank = jnp.int32(0)
    for other in owned:
        far = jnp.abs(other - z)
        nearer = (far < mine) | ((far == mine) & (other < block))
        rank = rank + nearer.astype(jnp.int32)
    return rank


def pick_ranked(owned, z, s):
    block = owned[0]
    for one in owned[1:]:
        block = jnp.where(rank_of(one, z, owned) == s, one, block)
    return block


def scalars(n, nb, cand, refs):
    pairs = [[refs[0, b * cand + k] for k in range(cand)] for b in range(nb)]
    return pairs, [refs[0, nb * cand + j] for j in range(n)]


def pick(values, index):
    got = values[0]
    for k in range(1, len(values)):
        got = jnp.where(index == k, values[k], got)
    return got


def listed(pairs, b, block):
    wanted = pairs[b][0] == block
    for one in pairs[b][1:]:
        wanted = wanted | (one == block)
    return wanted


def sources(dists, chunks, refs):
    z = lax.axis_index("blk")
    core = lax.axis_index("qry")
    at = 0
    found = []
    for d in dists:
        directions = (0,) if d == 0 else (-d, d)
        for there in directions:
            found.append((z + jnp.where(core == 0, -there, there), refs[at : at + chunks]))
            at += chunks
    return found


def fetch(block, pool, into, w_into, sems):
    feats = into.shape[1]
    for held, refs in pool:

        @pl.when(held == block)
        def _():
            at = 0
            for ref in refs:
                rows = ref if ref.shape[1] == feats else ref.at[:, pl.ds(0, feats)]
                pltpu.make_async_copy(rows, into.at[pl.ds(at, ref.shape[0])], sems.at[0]).start()
                at += ref.shape[0]
            tail = refs[-1].at[pl.ds(0, TAIL), pl.ds(feats, w_into.shape[1])]
            pltpu.make_async_copy(tail, w_into, sems.at[1]).start()


def fetched(into, w_into, sems):
    pltpu.make_async_copy(into, into, sems.at[0]).wait()
    pltpu.make_async_copy(w_into, w_into, sems.at[1]).wait()
    return w_into[...].astype(jnp.float32)[:1]


def dot_rows(a, b):
    return lax.dot_general(a, b, (((1,), (1,)), ((), ())), preferred_element_type=jnp.float32)


def coded(tile):
    top = jnp.maximum(jnp.max(jnp.abs(tile), axis=0, keepdims=True), 1e-36)
    power = jnp.ceil(jnp.log2(top))
    steps = jnp.clip(jnp.round(tile * jnp.exp2(-power) * STEPS), -STEPS, STEPS)
    return steps.astype(jnp.int32).astype(jnp.int16), power


def decoded(part, b, span, count):
    power = part[pl.ds(count, TAIL), :].astype(jnp.int32).astype(jnp.float32)[b : b + 1]
    steps = part[span, :].astype(jnp.int32).astype(jnp.float32)
    return steps * (jnp.exp2(power) * (1.0 / STEPS))


def put_coded(out, b, span, count, tile):
    steps, power = coded(tile)
    out[span, :] = steps
    line = lax.broadcasted_iota(jnp.int32, (TAIL, tile.shape[1]), 0)
    old = out[pl.ds(count, TAIL), :].astype(jnp.int32)
    out[pl.ds(count, TAIL), :] = jnp.where(line == b, power.astype(jnp.int32), old).astype(jnp.int16)


def score_slot(pairs, block, qs, rows, weight, out):
    qblk, count = qs[0].shape[0], len(qs) * qs[0].shape[0]
    out[pl.ds(count, TAIL), :] = jnp.zeros((TAIL, out.shape[1]), jnp.int16)
    for b in range(len(qs)):
        span = pl.ds(b * qblk, qblk)
        wanted = listed(pairs, b, block)

        @pl.when(wanted)
        def _():
            put_coded(out, b, span, count, dot_rows(qs[b][...], rows[...]) * weight)

        @pl.when(jnp.logical_not(wanted))
        def _():
            out[span, :] = jnp.zeros((qblk, out.shape[1]), jnp.int16)


def slot_kernel(sizes, s, dists, chunks, packed, *refs):
    n, ckpts, per, nb, cand = sizes
    qs, ins = refs[:nb], refs[nb : -(ckpts - 1) - 3]
    outs = refs[-(ckpts - 1) - 3 : -3]
    rows, w_rows, sems = refs[-3:]
    z, c = lax.axis_index("blk"), lax.axis_index("ckpt")
    pairs, order = scalars(n, nb, cand, packed)
    pool = sources(dists, chunks, ins)
    for r in range(1, ckpts):
        owner = lax.rem(c + r, ckpts)
        block = pick_ranked([pick(order[k::per], owner) for k in range(per)], z, s)

        @pl.when(jnp.abs(block - z) <= dists[-1])
        def _():
            fetch(block, pool, rows, w_rows, sems)
            weight = fetched(rows, w_rows, sems)
            score_slot(pairs, block, qs, rows, weight, outs[r - 1])


def late_kernel(sizes, s, dist, chunks, packed, *refs):
    n, ckpts, per, nb, cand = sizes
    qs, ins = refs[:nb], refs[nb : nb + 2 * chunks]
    before, outs, rows = refs[nb + 2 * chunks : -ckpts], refs[-ckpts:-1], refs[-1]
    z, c = lax.axis_index("blk"), lax.axis_index("ckpt")
    pairs, order = scalars(n, nb, cand, packed)
    feats = rows.shape[1]
    for r in range(1, ckpts):
        owner = lax.rem(c + r, ckpts)
        block = pick_ranked([pick(order[k::per], owner) for k in range(per)], z, s)
        late = jnp.abs(block - z) == dist

        @pl.when(late)
        def _():
            weight = jnp.zeros((1, outs[0].shape[1]), jnp.float32)
            for held, parts in sources((dist,), chunks, ins):

                @pl.when(held == block)
                def _():
                    at = 0
                    for part in parts:
                        rows[pl.ds(at, part.shape[0]), :] = part[:, pl.ds(0, feats)]
                        at += part.shape[0]

                tail = parts[-1][pl.ds(0, TAIL), pl.ds(feats, outs[0].shape[1])].astype(jnp.float32)[:1]
                weight = jnp.where(held == block, tail, weight)
            score_slot(pairs, block, qs, rows, weight, outs[r - 1])

        @pl.when(jnp.logical_not(late))
        def _():
            outs[r - 1][...] = before[r - 1][...]


def regroup(tiles, index, width):
    group = lax.broadcasted_iota(jnp.int32, tiles[0].shape, 1) // width
    total = jnp.zeros_like(tiles[0])
    for k, tile in enumerate(tiles):
        by = (k - index) * width % tile.shape[1]
        total = total + jnp.where(group == k, pltpu.roll(tile, by, 1) if by else tile, 0.0)
    return total


def put_piece(tiles, out, weight):
    qblk = tiles[0].shape[0]
    tail = jnp.broadcast_to(jnp.round(weight * WEIGHT_STEPS), (TAIL, weight.shape[1])).astype(jnp.int32)
    line = lax.broadcasted_iota(jnp.int32, tail.shape, 0)
    for k, tile in enumerate(tiles):
        steps, power = coded(tile)
        out[pl.ds(k * qblk, qblk), :] = steps
        tail = jnp.where(line == k, power.astype(jnp.int32), tail)
    out[pl.ds(len(tiles) * qblk, TAIL), :] = tail.astype(jnp.int16)


def packed_pieces(part_refs, nb, b):
    chunks, width = len(part_refs), part_refs[0].shape[1]
    groups, k = nb // chunks, b // chunks
    qblk = (part_refs[0].shape[0] - TAIL) // groups
    tails = [ref[pl.ds(groups * qblk, TAIL), :].astype(jnp.int32).astype(jnp.float32) for ref in part_refs]
    weight = tails[-1][TAIL - 1 :] * (1.0 / WEIGHT_STEPS)
    tiles = []
    for ref, tail in zip(part_refs, tails):
        steps = ref[pl.ds(k * qblk, qblk), :].astype(jnp.int32).astype(jnp.float32)
        tiles.append(steps * (jnp.exp2(tail[k : k + 1]) * (1.0 / STEPS)))
    return regroup(tiles, b % chunks, width // chunks) * weight


def far_kernel(sizes, dists, chunks, packed, *refs):
    n, ckpts, per, nb, cand = sizes
    many = (ckpts - 1) * chunks
    qs, ins, outs = refs[:nb], refs[nb : -many - 4], refs[-many - 4 : -4]
    rows, w_rows, tiles, sems = refs[-4:]
    z, c = lax.axis_index("blk"), lax.axis_index("ckpt")
    pairs, order = scalars(n, nb, cand, packed)
    pool = sources(dists, chunks, ins)
    for r in range(1, ckpts):
        owner = lax.rem(c + r, ckpts)
        block = pick_ranked([pick(order[k::per], owner) for k in range(per)], z, per - 1)

        @pl.when(jnp.abs(block - z) <= dists[-1])
        def _():
            fetch(block, pool, rows, w_rows, sems)
            weight = fetched(rows, w_rows, sems)
            score_tiles(pairs, block, qs, rows, tiles)
            for i in range(chunks):
                groups = [
                    regroup([tiles[k * chunks + j] for j in range(chunks)], i, rows.shape[0] // chunks)
                    for k in range(nb // chunks)
                ]
                put_piece(groups, outs[(r - 1) * chunks + i], weight)


def score_tiles(pairs, block, qs, rows, tiles):
    for b in range(len(qs)):
        wanted = listed(pairs, b, block)

        @pl.when(wanted)
        def _():
            tiles[b] = dot_rows(qs[b][...], rows[...])

        @pl.when(jnp.logical_not(wanted))
        def _():
            tiles[b] = jnp.zeros_like(tiles[b])


def piece_kernel(sizes, i, dist, chunks, packed, *refs):
    n, ckpts, per, nb, cand = sizes
    qs, ins = refs[:nb], refs[nb : nb + 2]
    before, outs = refs[nb + 2 : nb + 1 + ckpts], refs[nb + 1 + ckpts : -2]
    rows, tiles = refs[-2:]
    z, c = lax.axis_index("blk"), lax.axis_index("ckpt")
    pairs, order = scalars(n, nb, cand, packed)
    width, feats = rows.shape
    piece = width // chunks
    for r in range(1, ckpts):
        owner = lax.rem(c + r, ckpts)
        block = pick_ranked([pick(order[k::per], owner) for k in range(per)], z, per - 1)
        late = jnp.abs(block - z) == dist

        @pl.when(late)
        def _():
            weight = jnp.ones((1, width), jnp.float32)
            for held, (part,) in sources((dist,), 1, ins):

                @pl.when(held == block)
                def _():
                    for j in range(chunks):
                        rows[pl.ds(j * piece, piece), :] = part[:, pl.ds(0, feats)]

                if i == chunks - 1:
                    tag = part[pl.ds(0, TAIL), pl.ds(feats, width)].astype(jnp.float32)[:1]
                    weight = jnp.where(held == block, tag, weight)
            score_tiles(pairs, block, qs, rows, tiles)
            group = lax.broadcasted_iota(jnp.int32, tiles.shape[1:], 1) // piece
            groups = []
            for k in range(nb // chunks):
                total = tiles[k * chunks]
                for j in range(1, chunks):
                    total = jnp.where(group == j, tiles[k * chunks + j], total)
                groups.append(total)
            put_piece(groups, outs[r - 1], weight)

        @pl.when(jnp.logical_not(late))
        def _():
            outs[r - 1][...] = before[r - 1][...]


def own_kernel(sizes, dists, chunks, packed, *refs):
    n, ckpts, per, nb, cand = sizes
    early = (per - 1) * (ckpts - 1)
    qs, ins, came = refs[:nb], refs[nb : len(refs) - early - 6], refs[len(refs) - early - 6 : -6]
    out, last, rows, w_rows, tiles, sems = refs[-6:]
    z, c = lax.axis_index("blk"), lax.axis_index("ckpt")
    pairs, order = scalars(n, nb, cand, packed)
    qblk, width = qs[0].shape[0], rows.shape[1]
    count = nb * qblk
    pool = sources(dists, chunks, ins)
    owned = [pick(order[k::per], c) for k in range(per)]
    ranked = [pick_ranked(owned, z, s) for s in range(per)]
    for s, block in enumerate(ranked):
        fetch(block, pool, rows.at[s], w_rows.at[s], sems.at[s])
    for s, block in enumerate(ranked):
        weight = fetched(rows.at[s], w_rows.at[s], sems.at[s])
        into = last if s == per - 1 else tiles.at[s]
        for b in range(nb):
            span = pl.ds(b * qblk, qblk)
            wanted = listed(pairs, b, block)

            @pl.when(wanted)
            def _():
                total = dot_rows(qs[b][...], rows[s]) * weight
                if s < per - 1:
                    for r in range(ckpts - 1):
                        total = total + decoded(came[s * (ckpts - 1) + r], b, span, count)
                into[span, :] = total

            @pl.when(jnp.logical_not(wanted))
            def _():
                into[span, :] = jnp.zeros((qblk, width), jnp.float32)

        if s < per - 1:
            put_columns(tiles.at[s], out, owned, block, sems.at[s, 0]).start()
    for s, block in enumerate(ranked[:-1]):
        put_columns(tiles.at[s], out, owned, block, sems.at[s, 0]).wait()


def put_columns(tile, out, owned, block, sem, span=slice(None)):
    width = tile.shape[1]
    slot = jnp.int32(0)
    for j, one in enumerate(owned):
        slot = jnp.where(one == block, j, slot)
    columns = pl.ds(pl.multiple_of(slot * width, width), width)
    return pltpu.make_async_copy(tile.at[span, :], out.at[span, columns], sem)


def sum_kernel(sizes, packed, acc_ref, last_ref, *refs):
    n, ckpts, per, nb, cand = sizes
    came, out, tile, sems = refs[:-3], refs[-3], refs[-2], refs[-1]
    z, c = lax.axis_index("blk"), lax.axis_index("ckpt")
    _, order = scalars(n, nb, cand, packed)
    count = last_ref.shape[0]
    qblk = count // nb
    owned = [pick(order[k::per], c) for k in range(per)]
    block = pick_ranked(owned, z, per - 1)
    stores = []
    chunks = len(came) // (ckpts - 1)
    for b in range(nb):
        span = pl.ds(b * qblk, qblk)
        total = last_ref[span, :]
        for r in range(ckpts - 1):
            total = total + packed_pieces(came[r * chunks : (r + 1) * chunks], nb, b)
        tile[span, :] = total
        stores.append(put_columns(tile, out, owned, block, sems.at[b], span))
        stores[-1].start()
    for store in stores:
        store.wait()


def per_device(query_feats, train_feats, loss_weights, pair_list, tile_owner):
    queries, own_rows = query_feats[0], train_feats[0]
    n, ckpts = lax.axis_size("blk"), lax.axis_size("ckpt")
    per = n // ckpts
    rows, feats = own_rows.shape
    count = queries.shape[0]
    lines = ("blk", "qry")
    ring, swap = fold_ring(n), shift(2, 1)
    chunks = len(SPLIT)

    params = pltpu.CompilerParams(vmem_limit_bytes=LIMIT)
    nb, cand = pair_list.shape
    sizes = (n, ckpts, per, nb, cand)
    held = [own_rows[a : a + length] for a, length in cuts(rows)]
    tagged = jnp.broadcast_to(loss_weights, (held[-1].shape[0], rows))
    held[-1] = jnp.concatenate([held[-1], tagged], axis=1)
    packed = jnp.concatenate([pair_list.reshape(1, nb * cand), tile_owner[None, :]], axis=1)
    qblk = count // nb
    asked = []
    for b in range(nb):
        asked.append(queries[b * qblk : (b + 1) * qblk])
    near = {0: held}
    for step in range(1, n):
        held = [lax.ppermute(part, lines, ring) for part in held]
        near[step] = held + [lax.ppermute(part, "qry", swap) for part in held]
    sent = jax.ShapeDtypeStruct((count + TAIL, rows), jnp.int16)
    tile = jax.ShapeDtypeStruct((count, rows), jnp.float32)
    acc = jax.ShapeDtypeStruct((count, per * rows), jnp.float32)
    flops = 2 * count * rows * feats
    came = []
    cost = pl.CostEstimate(flops=flops * (ckpts - 1), bytes_accessed=count * feats * 2, transcendentals=0)
    for s in range(per - 1):
        seen = n - per + max(s - 1, 0)
        dists = tuple(range(seen + 1))
        pool = [ref for d in dists for ref in near[d]]
        terms = pl.pallas_call(
            functools.partial(slot_kernel, sizes, s, dists, chunks),
            out_shape=[sent] * (ckpts - 1),
            in_specs=[VMEM] + [VMEM] * nb + [ANY] * len(pool),
            out_specs=[VMEM] * (ckpts - 1),
            scratch_shapes=[
                pltpu.VMEM((rows, feats), jnp.bfloat16),
                pltpu.VMEM((TAIL, rows), jnp.bfloat16),
                pltpu.SemaphoreType.DMA((2,)),
            ],
            compiler_params=params,
            cost_estimate=cost,
        )(packed, *asked, *pool)
        if s > 0:
            terms = pl.pallas_call(
                functools.partial(late_kernel, sizes, s, seen + 1, chunks),
                out_shape=[sent] * (ckpts - 1),
                in_specs=[VMEM] + [VMEM] * (nb + 2 * chunks + ckpts - 1),
                out_specs=[VMEM] * (ckpts - 1),
                scratch_shapes=[pltpu.VMEM((rows, feats), jnp.bfloat16)],
                compiler_params=params,
                cost_estimate=cost,
            )(packed, *asked, *near[seen + 1], *terms)
        came.append([lax.ppermute(terms[r - 1], "ckpt", shift(ckpts, r)) for r in range(1, ckpts)])
    seen = n - 2
    dists = tuple(range(seen + 1))
    pool = [ref for d in dists for ref in near[d]]
    sent = jax.ShapeDtypeStruct((count // chunks + TAIL, rows), jnp.int16)
    tiles = pltpu.VMEM((nb, qblk, rows), jnp.float32)
    terms = pl.pallas_call(
        functools.partial(far_kernel, sizes, dists, chunks),
        out_shape=[sent] * ((ckpts - 1) * chunks),
        in_specs=[VMEM] * (1 + nb) + [ANY] * len(pool),
        out_specs=[VMEM] * ((ckpts - 1) * chunks),
        scratch_shapes=[
            pltpu.VMEM((rows, feats), jnp.bfloat16),
            pltpu.VMEM((TAIL, rows), jnp.bfloat16),
            tiles,
            pltpu.SemaphoreType.DMA((2,)),
        ],
        compiler_params=params,
        cost_estimate=cost,
    )(packed, *asked, *pool)
    pieces = {}
    for i in range(chunks):
        done = pl.pallas_call(
            functools.partial(piece_kernel, sizes, i, seen + 1, chunks),
            out_shape=[sent] * (ckpts - 1),
            in_specs=[VMEM] * (1 + nb + 2 + ckpts - 1),
            out_specs=[VMEM] * (ckpts - 1),
            scratch_shapes=[pltpu.VMEM((rows, feats), jnp.bfloat16), tiles],
            compiler_params=params,
            cost_estimate=cost,
        )(packed, *asked, near[seen + 1][i], near[seen + 1][chunks + i], *terms[i::chunks])
        for r in range(1, ckpts):
            pieces[r, i] = lax.ppermute(done[r - 1], "ckpt", shift(ckpts, r))
    came.append([pieces[r, i] for r in range(1, ckpts) for i in range(chunks)])
    dists = tuple(range(n))
    pool = [ref for d in dists for ref in near[d]]
    early = [part for parts in came[:-1] for part in parts]
    total, last = pl.pallas_call(
        functools.partial(own_kernel, sizes, dists, chunks),
        out_shape=[acc, tile],
        in_specs=[VMEM] + [VMEM] * nb + [ANY] * len(pool) + [VMEM] * len(early),
        out_specs=[ANY, VMEM],
        scratch_shapes=[
            pltpu.VMEM((per, rows, feats), jnp.bfloat16),
            pltpu.VMEM((per, TAIL, rows), jnp.bfloat16),
            pltpu.VMEM((max(per - 1, 1), count, rows), jnp.float32),
            pltpu.SemaphoreType.DMA((per, 2)),
        ],
        compiler_params=params,
        cost_estimate=pl.CostEstimate(flops=flops * per, bytes_accessed=count * feats * 2, transcendentals=0),
    )(packed, *asked, *pool, *early)
    return pl.pallas_call(
        functools.partial(sum_kernel, sizes),
        out_shape=acc,
        in_specs=[VMEM, ANY, VMEM] + [VMEM] * len(came[-1]),
        out_specs=ANY,
        input_output_aliases={1: 0},
        scratch_shapes=[pltpu.VMEM((count, rows), jnp.float32), pltpu.SemaphoreType.DMA((nb,))],
        compiler_params=params,
    )(packed, total, last, *came[-1])


def solution(mesh):
    return jax.shard_map(
        per_device,
        mesh=mesh,
        in_specs=(
            P("ckpt", ("shard", "blk", "qry"), None),
            P("ckpt", ("shard", "blk"), None),
            P("ckpt", ("shard", "blk")),
            P(("shard", "blk", "qry"), None),
            P("shard"),
        ),
        out_specs=P(("shard", "blk", "qry"), "ckpt"),
        check_vma=False,
    )
```
